32 devices in a mesh: space: 8 (over z, x), member: 4 (over y, core).
Axes of the slice: x: 2, y: 2, z: 4, core: 2. Of those that a mesh axis runs over, the one named last changes fastest.
Arguments:
- prediction_maps: bfloat16 [4, 72, 16, 1440], P('member', None, 'space'), may hold values from -6 to 6
- truth_analysis: float32 [72, 23040], P(None, ('space', 'member')), may hold values from -6 to 6
- reciprocal_spread: float32 [72], replicated, may hold values from 0.3 to 3
- deconv_inputs: bfloat16 [4, 72, 16, 1440], P('member', None, 'space'), may hold values from -6 to 6
- filter_tensor: bfloat16 [5, 5, 72, 72], replicated, may hold values from -0.125 to 0.125
Outputs:
- grad_hidden: bfloat16 [4, 72, 16, 1440], P('member', None, 'space')
- grad_kernel: float32 [5, 5, 72, 72], replicated
The draws below stay inside these ranges and needn't reach their ends.
All inputs are finite; a program needn't handle non-finite values.
Results may differ from the reference program's by a relative error of at most 0.018.
Values may be sent and summed in bfloat16 or wider, within the bound.
No kernel may reach another device: no remote copies, remote signals or barrier semaphores. Data moves between devices by JAX's collectives and lax.ppermute only.
A program may use at most 64 MiB of HBM per device.

```python
import math
import jax
import jax.numpy as jnp
from jax import lax

QUANTITY_TOTAL = 72
MERIDIAN_TOTAL = 1440
KW = 5
ENSEMBLE_SIZE = 4
PARALLEL_TOTAL = 16


def shard_levels(own_key, shape, cuts, smallest, largest):
    def one(position, parts):
        heights = jax.random.uniform(jax.random.fold_in(jax.random.fold_in(own_key, 6), position), (parts,), jnp.float32, smallest / len(cuts), largest / len(cuts))
        return jnp.repeat(jnp.exp(heights), shape[position] // parts).reshape((-1,) + (1,) * (len(shape) - position - 1))

    level = one(*cuts[0])
    for cut in cuts[1:]:
        level = level * one(*cut)
    return level


def normal_values(own_key, extent, width, most, cuts=(), kind=jnp.bfloat16):
    entries = jax.random.normal(own_key, extent, jnp.float32) * width
    if len(cuts) > 0:
        entries = shard_levels(own_key, extent, cuts, -0.22, 0.18) * entries
    return jnp.clip(entries, min=-most, max=most).astype(kind)


def setup_inputs(seed: int = 0) -> dict:
    key_list = jax.random.split(jax.random.key(seed), 6)
    prediction_maps = normal_values(key_list[0], (ENSEMBLE_SIZE, QUANTITY_TOTAL, PARALLEL_TOTAL, MERIDIAN_TOTAL), 1.0, 6.0, ((0, 4), (2, 8)))
    truth_analysis = normal_values(key_list[1], (QUANTITY_TOTAL, PARALLEL_TOTAL * MERIDIAN_TOTAL), 1.0, 6.0, ((1, 32),), jnp.float32)
    reciprocal_spread = jnp.clip(jnp.exp(jax.random.uniform(key_list[2], (QUANTITY_TOTAL,), jnp.float32, math.log(0.3), math.log(3.0))), 0.3, 3.0)
    deconv_inputs = normal_values(key_list[3], (ENSEMBLE_SIZE, QUANTITY_TOTAL, PARALLEL_TOTAL, MERIDIAN_TOTAL), 1.0, 6.0, ((0, 4), (2, 8)))
    filter_tensor = normal_values(key_list[4], (KW, KW, QUANTITY_TOTAL, QUANTITY_TOTAL), (KW * KW * QUANTITY_TOTAL) ** -0.5, 0.125)
    return dict(prediction_maps=prediction_maps, truth_analysis=truth_analysis, reciprocal_spread=reciprocal_spread, deconv_inputs=deconv_inputs, filter_tensor=filter_tensor)


smoothing = 1.0

def area_weights(rows_total):
    index = jnp.arange(rows_total, dtype=jnp.float32)
    latitude = (index + 0.5) * (jnp.pi / rows_total) - jnp.pi / 2
    cosine = jnp.cos(latitude)
    return cosine / jnp.mean(cosine)

def direct_term(own, target, scale):
    offset = scale * (own - target[None])
    radius = jnp.sqrt(lax.optimization_barrier(jnp.sum(offset * offset, axis=1, keepdims=True)) + smoothing)
    return scale * offset / radius

def pair_sums(scaled_own, scaled_other):
    own_sq = lax.optimization_barrier(jnp.sum(scaled_own * scaled_own, axis=1))
    other_sq = lax.optimization_barrier(jnp.sum(scaled_other * scaled_other, axis=1))
    inner = jnp.einsum('mcp,ncp->mnp', scaled_own, scaled_other, precision=lax.Precision.HIGHEST)
    spread_sq = own_sq[:, None, :] + other_sq[None, :, :] - 2.0 * inner + smoothing
    inverse = 1.0 / jnp.sqrt(spread_sq)
    total_weight = lax.optimization_barrier(jnp.sum(inverse, axis=1))
    mixture = jnp.einsum('mnp,ncp->mcp', inverse, scaled_other, precision=lax.Precision.HIGHEST)
    return (total_weight, mixture)

def reference(prediction_maps, truth_analysis, reciprocal_spread, deconv_inputs, filter_tensor):
    predicted_maps = prediction_maps.astype(jnp.float32).reshape(ENSEMBLE_SIZE, QUANTITY_TOTAL, PARALLEL_TOTAL * MERIDIAN_TOTAL)
    target = truth_analysis.reshape(QUANTITY_TOTAL, PARALLEL_TOTAL * MERIDIAN_TOTAL)
    scale = reciprocal_spread[None, :, None]
    direct = direct_term(predicted_maps, target, scale)
    scaled = scale * predicted_maps
    total_weight, mixture = pair_sums(scaled, scaled)
    paired = scale * (scaled * total_weight[:, None, :] - mixture)
    terms = (direct - paired / ENSEMBLE_SIZE).reshape(ENSEMBLE_SIZE, QUANTITY_TOTAL, PARALLEL_TOTAL, MERIDIAN_TOTAL)
    weights = area_weights(PARALLEL_TOTAL)
    grad_out = (terms * weights[None, None, :, None]).astype(jnp.bfloat16)

    def per_member(total, pair):
        member_grad, member_hidden = pair
        padded = jnp.pad(member_grad, ((0, 0), (2, 2), (0, 0)))
        wrapped = jnp.concatenate([padded[:, :, -2:], padded, padded[:, :, :2]], axis=2)
        flat_hidden = member_hidden.reshape(QUANTITY_TOTAL, PARALLEL_TOTAL * MERIDIAN_TOTAL)
        back = jnp.zeros((QUANTITY_TOTAL, PARALLEL_TOTAL * MERIDIAN_TOTAL), jnp.float32)
        pieces = []
        for row_shift in range(KW):
            for col_shift in range(KW):
                shifted = wrapped[:, row_shift:row_shift + PARALLEL_TOTAL, col_shift:col_shift + MERIDIAN_TOTAL].reshape(QUANTITY_TOTAL, PARALLEL_TOTAL * MERIDIAN_TOTAL)
                back = back + jnp.dot(filter_tensor[row_shift, col_shift], shifted, preferred_element_type=jnp.float32)
                pieces.append(jnp.dot(flat_hidden, shifted.T, preferred_element_type=jnp.float32))
        stacked = jnp.stack(pieces).reshape(KW, KW, QUANTITY_TOTAL, QUANTITY_TOTAL)
        return (total + stacked, back.astype(jnp.bfloat16).reshape(QUANTITY_TOTAL, PARALLEL_TOTAL, MERIDIAN_TOTAL))
    kernel_total, grad_hidden = lax.scan(per_member, jnp.zeros((KW, KW, QUANTITY_TOTAL, QUANTITY_TOTAL), jnp.float32), (grad_out, deconv_inputs))
    norm_factor = 1.0 / jnp.sqrt(jnp.float32(ENSEMBLE_SIZE * PARALLEL_TOTAL * MERIDIAN_TOTAL))
    return (grad_hidden, kernel_total * norm_factor)
```

```python
import functools

import jax
import jax.numpy as jnp
from jax import lax
from jax.experimental import pallas as pl
from jax.experimental.pallas import tpu as pltpu
from jax.sharding import Mesh, PartitionSpec as P

smoothing = 1.0
LANES = 128
BF = jnp.bfloat16
F32 = jnp.float32
VM = pl.BlockSpec(memory_space=pltpu.VMEM)
SM = pl.BlockSpec(memory_space=pltpu.SMEM)


def up(n, k):
    return -(-n // k) * k


def area_weights(rows_total):
    index = jnp.arange(rows_total, dtype=F32)
    latitude = (index + 0.5) * (jnp.pi / rows_total) - jnp.pi / 2
    cosine = jnp.cos(latitude)
    return cosine / jnp.mean(cosine)


def call(kernel, outs, ins, scratch=(), flops=0):
    nbytes = sum(x.size * x.dtype.itemsize for x in (*ins, *outs))
    return pl.pallas_call(
        kernel,
        out_shape=list(outs),
        in_specs=[SM if x.dtype == jnp.int32 else VM for x in ins],
        out_specs=[VM for _ in outs],
        scratch_shapes=list(scratch),
        cost_estimate=pl.CostEstimate(
            flops=flops, bytes_accessed=nbytes, transcendentals=0
        ),
        compiler_params=pltpu.CompilerParams(vmem_limit_bytes=40 << 20),
    )(*ins)


def lane_iota(shape):
    return lax.broadcasted_iota(jnp.int32, shape, len(shape) - 1)


def rows_kernel(width, half, x_ref, o_ref):
    rows = x_ref.shape[2]
    for r in range(rows):
        x = x_ref[0, :, r, :]
        o_ref[2 * r] = x[:, :half]
        tail = x[:, half:]
        o_ref[2 * r + 1] = jnp.concatenate(
            [tail, jnp.zeros((x.shape[0], 2 * half - width), x.dtype)], axis=1
        )


def fields_kernel(width, half, x_ref, t_ref, o_ref):
    rows_kernel(width, half, x_ref, o_ref)
    rows = x_ref.shape[2]
    t = t_ref[...].astype(o_ref.dtype)
    pieces = up(t.shape[1], half) // half
    for k in range(pieces):
        part = t[:, k * half : (k + 1) * half]
        if part.shape[1] < half:
            part = jnp.concatenate(
                [part, jnp.zeros((part.shape[0], half - part.shape[1]), part.dtype)],
                axis=1,
            )
        o_ref[2 * rows + k] = part


def energy_kernel(width, half, span, members, me_ref, w_ref, s_ref, *refs):
    others = refs[:members]
    o_ref, t_scr = refs[members:]
    rows = o_ref.shape[0]
    channels = o_ref.shape[1]
    parts = members // rows
    me = me_ref[0]
    for d in range(members):
        t_scr[me ^ d] = others[d][2 * rows][:, : t_scr.shape[2]]
    s = s_ref[...]
    for r in range(rows):
        truth = None
        for k in range(parts):
            piece = t_scr[r * parts + k].astype(F32)
            piece = jnp.concatenate(
                [piece, jnp.zeros((channels, 2 * half - piece.shape[1]), F32)], axis=1
            )
            if k:
                piece = pltpu.roll(piece, k * span, 1)
            truth = piece if truth is None else truth + piece
        weight = w_ref[r : r + 1, 0:1]
        for h in range(2):
            t = truth[:, h * half : (h + 1) * half]
            own = others[0][2 * r + h].astype(F32)
            scaled = s * own
            offset = scaled - s * t
            radius_sq = jnp.sum(offset * offset, axis=0, keepdims=True) + smoothing
            direct = offset * lax.rsqrt(radius_sq)
            self_inverse = 1.0 / jnp.sqrt(smoothing)
            total = self_inverse
            mixture = scaled * self_inverse
            for d in range(1, members):
                other = s * others[d][2 * r + h].astype(F32)
                diff = scaled - other
                spread_sq = jnp.sum(diff * diff, axis=0, keepdims=True) + smoothing
                inverse = lax.rsqrt(spread_sq)
                total = total + inverse
                mixture = mixture + other * inverse
            paired = scaled * total - mixture
            g = (weight * s) * (direct - paired * (1.0 / members))
            o_ref[r, :, h * half : (h + 1) * half] = g.astype(BF)
        last = (width // LANES) * LANES
        body = o_ref[r, :, last : last + LANES].astype(F32)
        head = o_ref[r, :, 0:LANES].astype(F32)
        lane = lane_iota(body.shape)
        off = width - last
        body = jnp.where(lane < off, body, 0.0)
        wrapped = jnp.where(
            (lane >= off) & (lane < off + 2), pltpu.roll(head, off, 1), body
        )
        tail = pltpu.roll(body, LANES - off, 1)
        wrapped = jnp.where(lane >= LANES - 2, tail, wrapped)
        o_ref[r, :, last : last + LANES] = wrapped.astype(BF)


def gather_rows(parity, own, near, far, scr):
    rows = scr.shape[0] // 3
    above, below = 2 * rows * (1 - parity), 2 * rows * parity
    for r in range(rows):
        scr[rows + r] = own(r)
        scr[above + r] = near(r)
        scr[below + r] = far(r)


def whole_row(ref):
    def get(r):
        return jnp.concatenate([ref[2 * r], ref[2 * r + 1]], axis=1)

    return get


def kgrad_kernel(ksize, par_ref, g_ref, own_ref, near_ref, far_ref, o_ref, h_scr, acc):
    rows, channels, lanes = g_ref.shape
    mid = ksize // 2
    gather_rows(
        par_ref[0], whole_row(own_ref), whole_row(near_ref), whole_row(far_ref), h_scr
    )
    total = None
    for r in range(rows):
        g = g_ref[r].astype(F32)
        shifted = jnp.concatenate(
            [
                (g if b == mid else pltpu.roll(g, (mid - b) % lanes, 1)).astype(BF)
                for b in range(ksize)
            ],
            axis=0,
        )
        h = h_scr[r : r + ksize].reshape(ksize * channels, lanes)
        part = lax.dot_general(
            h, shifted, (((1,), (1,)), ((), ())), preferred_element_type=F32
        )
        total = part if total is None else total + part
    n = ksize * channels
    o_ref[...] = jnp.zeros_like(o_ref)
    o_ref[:n, :n] = total.astype(o_ref.dtype)


def conv_kernel(ksize, width, par_ref, w_ref, own_ref, near_ref, far_ref, o_ref, g_scr):
    rows, channels, lanes = own_ref.shape
    mid = ksize // 2
    gather_rows(
        par_ref[0],
        lambda r: own_ref[r],
        lambda r: near_ref[r],
        lambda r: far_ref[r],
        g_scr,
    )
    w = w_ref[...]
    for r in range(rows):
        g = g_scr[r : r + ksize].reshape(ksize * channels, lanes)
        y = jnp.dot(w, g, preferred_element_type=F32)
        out = None
        for b in range(ksize):
            part = y[b * channels : (b + 1) * channels]
            if b != mid:
                part = pltpu.roll(part, (mid - b) % lanes, 1)
            out = part if out is None else out + part
        o_ref[r] = out[:, :width].astype(o_ref.dtype)


def final_kernel(ksize, channels, norm, x_ref, o_ref):
    for a in range(ksize):
        for b in range(ksize):
            i, j = (ksize - 1 - a) * channels, b * channels
            o_ref[a, b] = (
                x_ref[i : i + channels, j : j + channels].astype(F32) * norm
            )


def flip(x, axis, bit):
    size = lax.axis_size(axis)
    return lax.ppermute(x, axis, [(i, i ^ bit) for i in range(size)])


def along(x):
    size = lax.axis_size("space")
    pairs = [(i, i + 2) for i in range(0, size - 2, 2)]
    pairs += [(i, i - 2) for i in range(3, size, 2)]
    return lax.ppermute(x, "space", pairs)


def bits(axis):
    size, out = lax.axis_size(axis), []
    while (1 << len(out)) < size:
        out.append(1 << len(out))
    return out


def add(a, b):
    return (a.astype(F32) + b.astype(F32)).astype(BF)


def halve(x, axis):
    odd = lax.axis_index(axis) & 1
    n = x.shape[0] // 2
    keep = lax.dynamic_slice_in_dim(x, odd * n, n, 0)
    give = lax.dynamic_slice_in_dim(x, (1 - odd) * n, n, 0)
    return add(keep, flip(give, axis, 1))


def join(x, axis):
    odd = lax.axis_index(axis) & 1
    other = flip(x, axis, 1)
    both = jnp.concatenate([x, other], axis=0)
    swapped = jnp.concatenate([other, x], axis=0)
    return jnp.where(odd == 0, both, swapped)


def reduce_all(x):
    x = halve(x, "core")
    x = halve(x, "chip")
    for bit in bits("chip")[1:]:
        x = add(x, flip(x, "chip", bit))
    for bit in bits("space"):
        x = add(x, flip(x, "space", bit))
    return join(join(x, "chip"), "core")


def body(prediction_maps, truth_analysis, reciprocal_spread, deconv_inputs, filter_tensor):
    channels, rows, width = prediction_maps.shape[1:]
    ksize = filter_tensor.shape[0]
    chips = lax.axis_size("chip")
    members = chips * lax.axis_size("core")
    rows_total = rows * lax.axis_size("space")
    half = up(up(width + 4, LANES), 2 * LANES) // 2
    lanes = 2 * half
    span = truth_analysis.shape[1]
    space = lax.axis_index("space")
    me = lax.axis_index("chip") * 2 + lax.axis_index("core")
    parity = (space % 2).reshape(1)
    sds = jax.ShapeDtypeStruct
    weights = lax.dynamic_slice_in_dim(area_weights(rows_total), space * rows, rows)

    fields = call(
        functools.partial(fields_kernel, width, half),
        [sds((2 * rows + 1, channels, half), BF)],
        [prediction_maps, truth_analysis],
    )[0]
    have = [fields]
    for bit in bits("chip"):
        have += [flip(x, "chip", bit) for x in have]
    pairs = []
    for x in have:
        pairs += [x, flip(x, "core", 1)]

    hidden = call(
        functools.partial(rows_kernel, width, half),
        [sds((2 * rows, channels, half), BF)],
        [deconv_inputs],
    )[0]
    hidden_near = flip(hidden, "space", 1)
    hidden_far = along(hidden_near)
    taps = jnp.transpose(filter_tensor, (1, 2, 0, 3)).reshape(
        ksize * channels, ksize * channels
    )

    grad = call(
        functools.partial(energy_kernel, width, half, span, members),
        [sds((rows, channels, lanes), BF)],
        [
            me.reshape(1),
            jnp.broadcast_to(weights[:, None], (rows, LANES)),
            reciprocal_spread[:, None],
            *pairs,
        ],
        [pltpu.VMEM((members, channels, span), BF)],
    )[0]

    grad_near = flip(grad, "space", 1)
    grad_far = along(grad_near)

    n = ksize * channels
    packed = up(n, LANES)
    partial = call(
        functools.partial(kgrad_kernel, ksize),
        [sds((packed, packed), BF)],
        [parity, grad, hidden, hidden_near, hidden_far],
        [pltpu.VMEM((3 * rows, channels, lanes), BF), pltpu.VMEM((8, LANES), F32)],
        2 * n * n * rows * lanes,
    )[0]
    total = reduce_all(partial)

    back = call(
        functools.partial(conv_kernel, ksize, width),
        [sds((rows, channels, width), BF)],
        [parity, taps, grad, grad_near, grad_far],
        [pltpu.VMEM((3 * rows, channels, lanes), BF)],
        2 * n * n * rows * lanes,
    )[0]
    grad_hidden = jnp.transpose(back, (1, 0, 2))[None]

    norm = 1.0 / float(members * rows_total * width) ** 0.5
    grad_kernel = call(
        functools.partial(final_kernel, ksize, channels, norm),
        [sds((ksize, ksize, channels, channels), F32)],
        [total],
    )[0]
    return (grad_hidden, grad_kernel)


def solution(mesh):
    space, members = mesh.devices.shape
    fine = Mesh(
        mesh.devices.reshape(space, members // 2, 2), ("space", "chip", "core")
    )
    member = ("chip", "core")
    return jax.shard_map(
        body,
        mesh=fine,
        in_specs=(
            P(member, None, "space", None),
            P(None, ("space", *member)),
            P(),
            P(member, None, "space", None),
            P(),
        ),
        out_specs=(P(member, None, "space", None), P()),
        check_vma=False,
    )
```

```python
import functools

import jax
import jax.numpy as jnp
import numpy as np
from jax import lax
from jax.experimental import pallas as pl
from jax.experimental.pallas import tpu as pltpu
from jax.sharding import Mesh, PartitionSpec as P


smoothing = 1.0
LANES = 128
BF = jnp.bfloat16
F32 = jnp.float32
VM = pl.BlockSpec(memory_space=pltpu.VMEM)
ANY = pl.BlockSpec(memory_space=pl.ANY)


def up(n, k):
    return -(-n // k) * k


def area_weights(rows_total):
    index = np.arange(rows_total)
    latitude = (index + 0.5) * (np.pi / rows_total) - np.pi / 2
    cosine = np.cos(latitude)
    return cosine / np.mean(cosine)


def call(kernel, outs, ins, scratch=(), flops=0, anywhere=()):
    nbytes = sum(x.size * x.dtype.itemsize for x in (*ins, *outs))
    return pl.pallas_call(
        kernel,
        out_shape=list(outs),
        in_specs=[ANY if i in anywhere else VM for i in range(len(ins))],
        out_specs=[VM for _ in outs],
        scratch_shapes=list(scratch),
        cost_estimate=pl.CostEstimate(
            flops=flops, bytes_accessed=nbytes, transcendentals=0
        ),
        compiler_params=pltpu.CompilerParams(vmem_limit_bytes=16 << 20),
    )(*ins)


def lane_iota(shape):
    return lax.broadcasted_iota(jnp.int32, shape, len(shape) - 1)


def mixed(ref):
    x = ref[0]
    return x.reshape(x.shape[0] * x.shape[1], x.shape[2])


def scale_kernel(rows, s_ref, o_ref):
    n, c = o_ref.shape[0], s_ref.shape[1]
    i = lax.broadcasted_iota(jnp.int32, (n, c), 0)
    j = lax.broadcasted_iota(jnp.int32, (n, c), 1)
    s = jnp.where(i // rows == j, jnp.broadcast_to(s_ref[...], (n, c)), 0.0)
    s = jnp.sum(s, axis=1, keepdims=True)
    o_ref[...] = jnp.broadcast_to(s * s, o_ref.shape)


def pick(table, index):
    out = jnp.float32(table[0])
    for i, v in enumerate(table[1:], 1):
        out = jnp.where(index == i, jnp.float32(v), out)
    return out


def energy_kernel(span, members, weights, s_ref, *refs):
    fields, truths = refs[:members], refs[members : 2 * members]
    o_ref, part_scr, mix_scr, truth, grad, sem = refs[2 * members :]
    rows, channels, lanes = o_ref.shape
    width = fields[0].shape[3]
    mix = channels * rows
    parts = members // rows
    me = lax.axis_index("chip") * 2 + lax.axis_index("core")
    first = lax.axis_index("space") * rows
    copies = [
        pltpu.make_async_copy(truths[d], part_scr.at[me ^ d], sem.at[d])
        for d in range(members)
    ]
    for copy in copies:
        copy.start()
    for d in range(members):
        mix_scr[d] = mixed(fields[d])
    for copy in copies:
        copy.wait()
    i = lax.broadcasted_iota(jnp.int32, (mix, channels), 0)
    j = lax.broadcasted_iota(jnp.int32, (mix, channels), 1)
    place = [(i == j * rows + r).astype(BF) for r in range(rows)]
    for k in range(parts):
        truth[:, k * span : (k + 1) * span] = sum(
            jnp.dot(place[r], part_scr[r * parts + k], preferred_element_type=F32)
            for r in range(rows)
        )

    def sums(x):
        x = jnp.sum(x, axis=0)
        step = rows
        while step < 8:
            x = x + pltpu.roll(x, step, 0)
            step *= 2
        return x

    def load(d, low, high):
        x = mix_scr[d, :, low:high].astype(F32)
        return x.reshape(mix // 8, 8, high - low)

    sub = lax.broadcasted_iota(jnp.int32, (8, LANES), 0) % rows
    weight = pick(weights, first)
    pattern = jnp.full((8, LANES), weight, F32)
    for r in range(1, rows):
        pattern = jnp.where(sub == r, pick(weights, first + r), pattern)
    grad[width // LANES] = jnp.zeros((mix, LANES), F32)
    for low in range(0, width, LANES):
        high = min(low + LANES, width)
        n = high - low
        sq = s_ref[:, :n].reshape(mix // 8, 8, n)
        own = load(0, low, high)
        offset = own - truth[:, low:high].reshape(mix // 8, 8, n)
        direct = lax.rsqrt(sums(offset * offset * sq) + smoothing)
        self_inverse = 1.0 / jnp.sqrt(smoothing)
        total = jnp.full((8, n), self_inverse, F32)
        mixture = own * self_inverse
        for d in range(1, members):
            other = load(d, low, high)
            diff = own - other
            inverse = lax.rsqrt(sums(diff * diff * sq) + smoothing)
            total = total + inverse
            mixture = mixture + other * inverse[None]
        paired = own * total[None] - mixture
        g = offset * direct[None] - paired * (1.0 / members)
        g = g * (sq * pattern[None, :, :n])
        grad[low // LANES, :, :n] = g.reshape(mix, n)
    last = width // LANES
    body, head = grad[last], grad[0]
    lane = lane_iota(body.shape)
    off = width - last * LANES
    wrapped = jnp.where(
        (lane >= off) & (lane < off + 2), pltpu.roll(head, off, 1), body
    )
    tail = pltpu.roll(body, LANES - off, 1)
    grad[last] = jnp.where(lane >= LANES - 2, tail, wrapped)
    for r in range(rows):
        for tile in range(lanes // LANES):
            g = grad[tile, pl.ds(r, channels, stride=rows), :]
            o_ref[r, :, tile * LANES : (tile + 1) * LANES] = g.astype(BF)


def over_lanes(h, shifted):
    rows, n, _ = shifted.shape
    s = shifted[...].reshape(rows * n, shifted.shape[2])[:, : h.shape[1]]
    return lax.dot_general(h, s, (((1,), (1,)), ((), ())), preferred_element_type=F32)


def kgrad_own_kernel(ksize, g_ref, own_ref, shift_ref, o_ref):
    rows, channels, lanes = g_ref.shape
    mid = ksize // 2
    for r in range(rows):
        g = g_ref[r].astype(F32)
        for b in range(ksize):
            moved = g if b == mid else pltpu.roll(g, (mid - b) % lanes, 1)
            shift_ref[r, b * channels : (b + 1) * channels] = moved.astype(BF)
        rest = shift_ref.shape[1] - ksize * channels
        shift_ref[r, ksize * channels :] = jnp.zeros((rest, lanes), BF)
    o_ref[...] = over_lanes(mixed(own_ref), shift_ref)


def kgrad_kernel(ksize, shift_ref, own_ref, near_ref, far_ref, o_ref, acc):
    channels, rows = near_ref.shape[1:3]
    n = shift_ref.shape[1]
    odd = lax.axis_index("space") % 2
    mix = rows * channels
    both = over_lanes(
        jnp.concatenate([mixed(near_ref), mixed(far_ref)], axis=0), shift_ref
    )
    near, far = 2 * (1 - odd), 2 * odd
    for t in range(acc.shape[1]):
        lanes = slice(t * LANES, (t + 1) * LANES)
        acc[1, t] = own_ref[:, lanes]
        acc[near, t] = both[:mix, lanes]
        acc[far, t] = both[mix:, lanes]
    for i in range(ksize):
        for t in range(n // LANES):
            tap = None
            for r in range(rows):
                band, row = divmod(rows - ksize // 2 + r + i, rows)
                part = acc[
                    band, r * (n // LANES) + t, pl.ds(row, channels, stride=rows), :
                ]
                tap = part if tap is None else tap + part
            o_ref[
                i * channels : (i + 1) * channels, t * LANES : (t + 1) * LANES
            ] = tap.astype(o_ref.dtype)
    used = ksize * channels
    o_ref[used:] = jnp.zeros((o_ref.shape[0] - used, n), o_ref.dtype)


def gather_rows(own, near, far, scr):
    rows = scr.shape[0] // 3
    odd = lax.axis_index("space") % 2
    above, below = 2 * rows * (1 - odd), 2 * rows * odd
    for r in range(rows):
        scr[rows + r] = own(r)
        scr[above + r] = near(r)
        scr[below + r] = far(r)


def conv_kernel(ksize, w_ref, own_ref, near_ref, far_ref, o_ref, g_scr):
    rows, channels, lanes = own_ref.shape
    width = o_ref.shape[2]
    mid = ksize // 2
    gather_rows(
        lambda r: own_ref[r], lambda r: near_ref[r], lambda r: far_ref[r], g_scr
    )
    w = w_ref[...]
    for r in range(rows):
        g = g_scr[r : r + ksize].reshape(ksize * channels, lanes)
        y = jnp.dot(w, g, preferred_element_type=F32)
        out = None
        for b in range(ksize):
            part = y[b * channels : (b + 1) * channels]
            if b != mid:
                part = pltpu.roll(part, (mid - b) % lanes, 1)
            out = part if out is None else out + part
        o_ref[r] = out[:, :width].astype(o_ref.dtype)


def final_kernel(ksize, channels, norm, x_ref, o_ref):
    for a in range(ksize):
        for b in range(ksize):
            i, j = (ksize - 1 - a) * channels, b * channels
            o_ref[a, b] = (
                x_ref[i : i + channels, j : j + channels].astype(F32) * norm
            )


def flip(x, axis, bit):
    size = lax.axis_size(axis)
    return lax.ppermute(x, axis, [(i, i ^ bit) for i in range(size)])


def across(x):
    size = lax.axis_size("space")
    pairs = [(i, i + 1) for i in range(1, size - 1, 2)]
    pairs += [(i, i - 1) for i in range(2, size, 2)]
    return lax.ppermute(x, "space", pairs)


def bits(axis):
    size, out = lax.axis_size(axis), []
    while (1 << len(out)) < size:
        out.append(1 << len(out))
    return out


def add(a, b):
    return (a.astype(F32) + b.astype(F32)).astype(BF)


def halve(x, axis):
    odd = lax.axis_index(axis) & 1
    n = x.shape[0] // 2
    keep = lax.dynamic_slice_in_dim(x, odd * n, n, 0)
    give = lax.dynamic_slice_in_dim(x, (1 - odd) * n, n, 0)
    return add(keep, flip(give, axis, 1))


def join(x, axis):
    odd = lax.axis_index(axis) & 1
    other = flip(x, axis, 1)
    both = jnp.concatenate([x, other], axis=0)
    swapped = jnp.concatenate([other, x], axis=0)
    return jnp.where(odd == 0, both, swapped)


def reduce_all(x):
    x = halve(x, "core")
    x = halve(x, "chip")
    for bit in bits("chip")[1:]:
        x = add(x, flip(x, "chip", bit))
    for bit in bits("space")[1:] + [1]:
        x = add(x, flip(x, "space", bit))
    x = join(x, "chip")
    return join(x, "core")


def body(prediction_maps, truth_analysis, reciprocal_spread, deconv_inputs, filter_tensor):
    channels, rows, width = prediction_maps.shape[1:]
    ksize = filter_tensor.shape[0]
    members = lax.axis_size("chip") * lax.axis_size("core")
    rows_total = rows * lax.axis_size("space")
    lanes = up(width + 4, LANES)
    span = truth_analysis.shape[1]
    sds = jax.ShapeDtypeStruct
    slab = sds((rows, channels, lanes), BF)
    scratch = [pltpu.VMEM((3 * rows, channels, lanes), BF)]

    def core(x):
        return flip(x, "core", 1)

    def spread(x):
        have = [x]
        for bit in bits("chip"):
            have += [flip(h, "chip", bit) for h in have]
        return have

    fields = spread(prediction_maps)
    hidden_near = flip(deconv_inputs, "space", 1)
    truth = truth_analysis.astype(BF)
    truths = spread(truth)
    hidden_far = across(deconv_inputs)
    scale = call(
        functools.partial(scale_kernel, rows),
        [sds((rows * channels, LANES), F32)],
        [reciprocal_spread[None]],
    )[0]
    taps = jnp.transpose(filter_tensor, (1, 2, 0, 3)).reshape(
        ksize * channels, ksize * channels
    )
    arrived, seen = [], []
    for x, t in zip(fields, truths):
        arrived += [x, core(x)]
        seen += [t, core(t)]

    table = [float(v) for v in area_weights(rows_total)]
    grad = call(
        functools.partial(energy_kernel, span, members, table),
        [slab],
        [scale, *arrived, *seen],
        [
            pltpu.VMEM((members, channels, span), BF),
            pltpu.VMEM((members, rows * channels, width), BF),
            pltpu.VMEM((rows * channels, lanes), F32),
            pltpu.VMEM((lanes // LANES, rows * channels, LANES), F32),
            pltpu.SemaphoreType.DMA((members,)),
        ],
        anywhere=range(1 + members, 1 + 2 * members),
    )[0]

    grad_near = flip(grad, "space", 1)
    grad_far = across(grad)

    n = ksize * channels
    packed = up(n, LANES)
    flops = 2 * n * n * rows * lanes
    mix = rows * channels
    shifted, own_part = call(
        functools.partial(kgrad_own_kernel, ksize),
        [sds((rows, packed, lanes), BF), sds((mix, rows * packed), F32)],
        [grad, deconv_inputs],
        flops=flops // 3,
    )
    partial = call(
        functools.partial(kgrad_kernel, ksize),
        [sds((packed, packed), BF)],
        [shifted, own_part, hidden_near, hidden_far],
        [pltpu.VMEM((3, rows * packed // LANES, mix, LANES), F32)],
        flops * 2 // 3,
    )[0]
    total = reduce_all(partial)

    back = call(
        functools.partial(conv_kernel, ksize),
        [sds((rows, channels, width), BF)],
        [taps, grad, grad_near, grad_far],
        scratch,
        2 * n * n * rows * lanes,
    )[0]
    grad_hidden = jnp.transpose(back, (1, 0, 2))[None]

    norm = 1.0 / float(members * rows_total * width) ** 0.5
    grad_kernel = call(
        functools.partial(final_kernel, ksize, channels, norm),
        [sds((ksize, ksize, channels, channels), F32)],
        [total],
    )[0]
    return (grad_hidden, grad_kernel)


def solution(mesh):
    space, members = mesh.devices.shape
    fine = Mesh(
        mesh.devices.reshape(space, members // 2, 2), ("space", "chip", "core")
    )
    member = ("chip", "core")

    return jax.shard_map(
        body,
        mesh=fine,
        in_specs=(
            P(member, None, "space", None),
            P(None, ("space", *member)),
            P(),
            P(member, None, "space", None),
            P(),
        ),
        out_specs=(P(member, None, "space", None), P()),
        check_vma=False,
    )
```

```python
import functools
import math

import jax
import jax.numpy as jnp
import numpy as np
from jax import lax
from jax.experimental import pallas as pl
from jax.experimental.pallas import tpu as pltpu
from jax.sharding import Mesh, PartitionSpec as P


smoothing = 1.0
LANES = 128
BF = jnp.bfloat16
F32 = jnp.float32
VM = pl.BlockSpec(memory_space=pltpu.VMEM)
ANY = pl.BlockSpec(memory_space=pltpu.HBM)


def up(n, k):
    return -(-n // k) * k


def area_weights(rows_total):
    index = np.arange(rows_total)
    latitude = (index + 0.5) * (np.pi / rows_total) - np.pi / 2
    cosine = np.cos(latitude)
    return cosine / np.mean(cosine)


def call(kernel, outs, ins, scratch=(), flops=0, anywhere=(), outside=False, spare=3 << 20):
    nbytes = sum(x.size * x.dtype.itemsize for x in (*ins, *outs))
    held = sum(
        up(s.shape[-1], LANES) * math.prod(s.shape[:-1]) * s.dtype.itemsize
        for s in scratch
        if s.memory_space == pltpu.VMEM
    )
    return pl.pallas_call(
        kernel,
        out_shape=list(outs),
        in_specs=[ANY if i in anywhere else VM for i in range(len(ins))],
        out_specs=[ANY if outside else VM for _ in outs],
        scratch_shapes=list(scratch),
        cost_estimate=pl.CostEstimate(
            flops=flops, bytes_accessed=nbytes, transcendentals=0
        ),
        compiler_params=pltpu.CompilerParams(vmem_limit_bytes=held + spare),
    )(*ins)


def lane_iota(shape):
    return lax.broadcasted_iota(jnp.int32, shape, len(shape) - 1)


def mixed(ref):
    x = ref[0]
    return x.reshape(x.shape[0] * x.shape[1], x.shape[2])


def scale_kernel(rows, s_ref, o_ref):
    n, c = o_ref.shape[0], s_ref.shape[1]
    i = lax.broadcasted_iota(jnp.int32, (n, c), 0)
    j = lax.broadcasted_iota(jnp.int32, (n, c), 1)
    s = jnp.where(i // rows == j, jnp.broadcast_to(s_ref[...], (n, c)), 0.0)
    s = jnp.sum(s, axis=1, keepdims=True)
    o_ref[...] = jnp.broadcast_to(s * s, o_ref.shape)


def pick(table, index):
    out = jnp.float32(table[0])
    for i, v in enumerate(table[1:], 1):
        out = jnp.where(index == i, jnp.float32(v), out)
    return out


def energy_kernel(span, members, weights, s_ref, *refs):
    fields, truths = refs[:members], refs[members : 2 * members]
    o_ref, part_scr, mix_scr, truth, grad, sem = refs[2 * members :]
    rows, channels, lanes = o_ref.shape
    width = fields[0].shape[3]
    mix = channels * rows
    parts = members // rows
    me = lax.axis_index("chip") * 2 + lax.axis_index("core")
    first = lax.axis_index("space") * rows
    copies = [
        pltpu.make_async_copy(truths[d], part_scr.at[me ^ d], sem.at[d])
        for d in range(members)
    ]
    for copy in copies:
        copy.start()
    for d in range(members):
        mix_scr[d] = mixed(fields[d])
    for copy in copies:
        copy.wait()
    i = lax.broadcasted_iota(jnp.int32, (mix, channels), 0)
    j = lax.broadcasted_iota(jnp.int32, (mix, channels), 1)
    place = [(i == j * rows + r).astype(BF) for r in range(rows)]
    for k in range(parts):
        truth[:, k * span : (k + 1) * span] = sum(
            jnp.dot(place[r], part_scr[r * parts + k], preferred_element_type=F32)
            for r in range(rows)
        )

    def sums(x):
        x = jnp.sum(x, axis=0)
        step = rows
        while step < 8:
            x = x + pltpu.roll(x, step, 0)
            step *= 2
        return x

    def load(d, low, high):
        x = mix_scr[d, :, low:high].astype(F32)
        return x.reshape(mix // 8, 8, high - low)

    sub = lax.broadcasted_iota(jnp.int32, (8, LANES), 0) % rows
    weight = pick(weights, first)
    pattern = jnp.full((8, LANES), weight, F32)
    for r in range(1, rows):
        pattern = jnp.where(sub == r, pick(weights, first + r), pattern)
    grad[width // LANES] = jnp.zeros((mix, LANES), F32)
    for low in range(0, width, LANES):
        high = min(low + LANES, width)
        n = high - low
        sq = s_ref[:, :n].reshape(mix // 8, 8, n)
        own = load(0, low, high)
        offset = own - truth[:, low:high].reshape(mix // 8, 8, n)
        direct = lax.rsqrt(sums(offset * offset * sq) + smoothing)
        self_inverse = 1.0 / jnp.sqrt(smoothing)
        total = jnp.full((8, n), self_inverse, F32)
        mixture = own * self_inverse
        for d in range(1, members):
            other = load(d, low, high)
            diff = own - other
            inverse = lax.rsqrt(sums(diff * diff * sq) + smoothing)
            total = total + inverse
            mixture = mixture + other * inverse[None]
        paired = own * total[None] - mixture
        g = offset * direct[None] - paired * (1.0 / members)
        g = g * (sq * pattern[None, :, :n])
        grad[low // LANES, :, :n] = g.reshape(mix, n)
    last = width // LANES
    body, head = grad[last], grad[0]
    lane = lane_iota(body.shape)
    off = width - last * LANES
    wrapped = jnp.where(
        (lane >= off) & (lane < off + 2), pltpu.roll(head, off, 1), body
    )
    tail = pltpu.roll(body, LANES - off, 1)
    grad[last] = jnp.where(lane >= LANES - 2, tail, wrapped)
    for r in range(rows):
        for tile in range(lanes // LANES):
            g = grad[tile, pl.ds(r, channels, stride=rows), :]
            o_ref[r, :, tile * LANES : (tile + 1) * LANES] = g.astype(BF)


def over_lanes(h, shifted):
    rows, n, _ = shifted.shape
    s = shifted[...].reshape(rows * n, shifted.shape[2])[:, : h.shape[1]]
    return lax.dot_general(h, s, (((1,), (1,)), ((), ())), preferred_element_type=F32)


def kgrad_own_kernel(ksize, g_ref, own_ref, shift_ref, o_ref):
    rows, channels, lanes = g_ref.shape
    mid = ksize // 2
    for r in range(rows):
        g = g_ref[r].astype(F32)
        for b in range(ksize):
            moved = g if b == mid else pltpu.roll(g, (mid - b) % lanes, 1)
            shift_ref[r, b * channels : (b + 1) * channels] = moved.astype(BF)
        rest = shift_ref.shape[1] - ksize * channels
        shift_ref[r, ksize * channels :] = jnp.zeros((rest, lanes), BF)
    o_ref[...] = over_lanes(mixed(own_ref), shift_ref)


def kgrad_kernel(ksize, shift_ref, own_ref, near_ref, far_ref, o_ref, acc):
    channels, rows = near_ref.shape[1:3]
    n = shift_ref.shape[1]
    odd = lax.axis_index("space") % 2
    mix = rows * channels
    both = over_lanes(
        jnp.concatenate([mixed(near_ref), mixed(far_ref)], axis=0), shift_ref
    )
    near, far = 2 * (1 - odd), 2 * odd
    for t in range(acc.shape[1]):
        lanes = slice(t * LANES, (t + 1) * LANES)
        acc[1, t] = own_ref[:, lanes]
        acc[near, t] = both[:mix, lanes]
        acc[far, t] = both[mix:, lanes]
    for i in range(ksize):
        for t in range(n // LANES):
            tap = None
            for r in range(rows):
                band, row = divmod(rows - ksize // 2 + r + i, rows)
                part = acc[
                    band, r * (n // LANES) + t, pl.ds(row, channels, stride=rows), :
                ]
                tap = part if tap is None else tap + part
            o_ref[
                i * channels : (i + 1) * channels, t * LANES : (t + 1) * LANES
            ] = tap.astype(o_ref.dtype)
    used = ksize * channels
    o_ref[used:] = jnp.zeros((o_ref.shape[0] - used, n), o_ref.dtype)


def gather_rows(own, near, far, scr):
    rows = scr.shape[0] // 3
    odd = lax.axis_index("space") % 2
    above, below = 2 * rows * (1 - odd), 2 * rows * odd
    for r in range(rows):
        scr[rows + r] = own(r)
        scr[above + r] = near(r)
        scr[below + r] = far(r)


def conv_kernel(ksize, w_ref, own_ref, near_ref, far_ref, o_ref, g_scr):
    rows, channels, lanes = own_ref.shape
    width = o_ref.shape[2]
    mid = ksize // 2
    gather_rows(
        lambda r: own_ref[r], lambda r: near_ref[r], lambda r: far_ref[r], g_scr
    )
    w = w_ref[...]
    for r in range(rows):
        g = g_scr[r : r + ksize].reshape(ksize * channels, lanes)
        y = jnp.dot(w, g, preferred_element_type=F32)
        out = None
        for b in range(ksize):
            part = y[b * channels : (b + 1) * channels]
            if b != mid:
                part = pltpu.roll(part, (mid - b) % lanes, 1)
            out = part if out is None else out + part
        o_ref[r] = out[:, :width].astype(o_ref.dtype)


def final_kernel(ksize, channels, norm, x_ref, o_ref, scr, sem):
    copies = []
    for a in range(ksize):
        i = (ksize - 1 - a) * channels
        for b in range(ksize):
            j = b * channels
            scr[a, b] = x_ref[i : i + channels, j : j + channels].astype(F32) * norm
        copies.append(pltpu.make_async_copy(scr.at[a], o_ref.at[a], sem.at[a]))
        copies[-1].start()
    for copy in copies:
        copy.wait()


def flip(x, axis, bit):
    size = lax.axis_size(axis)
    return lax.ppermute(x, axis, [(i, i ^ bit) for i in range(size)])


def along(x):
    size = lax.axis_size("space")
    pairs = [(i, i + 2) for i in range(0, size - 2, 2)]
    pairs += [(i, i - 2) for i in range(3, size, 2)]
    return lax.ppermute(x, "space", pairs)


def across(x):
    size = lax.axis_size("space")
    pairs = [(i, i + 1) for i in range(1, size - 1, 2)]
    pairs += [(i, i - 1) for i in range(2, size, 2)]
    return lax.ppermute(x, "space", pairs)


def bits(axis):
    size, out = lax.axis_size(axis), []
    while (1 << len(out)) < size:
        out.append(1 << len(out))
    return out


def add(a, b):
    return (a.astype(F32) + b.astype(F32)).astype(BF)


def own_bit(axis, bit):
    return (lax.axis_index(axis) // bit) & 1


def halve(x, axis, bit):
    high = own_bit(axis, bit)
    n = x.shape[0] // 2
    keep = lax.dynamic_slice_in_dim(x, high * n, n, 0)
    give = lax.dynamic_slice_in_dim(x, (1 - high) * n, n, 0)
    return add(keep, flip(give, axis, bit))


def join(x, axis, bit):
    other = flip(x, axis, bit)
    both = jnp.concatenate([x, other], axis=0)
    swapped = jnp.concatenate([other, x], axis=0)
    return jnp.where(own_bit(axis, bit) == 0, both, swapped)


def reduce_all(x):
    core, first = ("core", 1), ("space", 2)
    x = halve(x, *core)
    x = halve(x, *first)
    rest = [("space", b) for b in bits("space")[2:]]
    rest += [("chip", b) for b in bits("chip")] + [("space", 1)]
    for axis in rest:
        x = add(x, flip(x, *axis))
    x = join(x, *first)
    return join(x, *core)


def body(prediction_maps, truth_analysis, reciprocal_spread, deconv_inputs, filter_tensor):
    channels, rows, width = prediction_maps.shape[1:]
    ksize = filter_tensor.shape[0]
    members = lax.axis_size("chip") * lax.axis_size("core")
    rows_total = rows * lax.axis_size("space")
    lanes = up(width + 4, LANES)
    span = truth_analysis.shape[1]
    sds = jax.ShapeDtypeStruct
    slab = sds((rows, channels, lanes), BF)
    scratch = [pltpu.VMEM((3 * rows, channels, lanes), BF)]

    def core(x):
        return flip(x, "core", 1)

    def spread(x):
        have = [x]
        for bit in bits("chip"):
            have += [flip(h, "chip", bit) for h in have]
        return have

    fields = spread(prediction_maps)
    hidden_near = flip(deconv_inputs, "space", 1)
    truth = truth_analysis.astype(BF)
    truths = spread(truth)
    hidden_far = across(deconv_inputs)
    scale = call(
        functools.partial(scale_kernel, rows),
        [sds((rows * channels, LANES), F32)],
        [reciprocal_spread[None]],
    )[0]
    taps = jnp.transpose(filter_tensor, (1, 2, 0, 3)).reshape(
        ksize * channels, ksize * channels
    )
    arrived, seen = [], []
    for x, t in zip(fields, truths):
        arrived += [x, core(x)]
        seen += [t, core(t)]

    table = [float(v) for v in area_weights(rows_total)]
    grad = call(
        functools.partial(energy_kernel, span, members, table),
        [slab],
        [scale, *arrived, *seen],
        [
            pltpu.VMEM((members, channels, span), BF),
            pltpu.VMEM((members, rows * channels, width), BF),
            pltpu.VMEM((rows * channels, lanes), F32),
            pltpu.VMEM((lanes // LANES, rows * channels, LANES), F32),
            pltpu.SemaphoreType.DMA((members,)),
        ],
        anywhere=range(1 + members, 1 + 2 * members),
        spare=max(3, members) << 20,
    )[0]

    grad_near = flip(grad, "space", 1)
    grad_far = along(grad_near)

    n = ksize * channels
    packed = up(n, LANES)
    flops = 2 * n * n * rows * lanes
    mix = rows * channels
    shifted, own_part = call(
        functools.partial(kgrad_own_kernel, ksize),
        [sds((rows, packed, lanes), BF), sds((mix, rows * packed), F32)],
        [grad, deconv_inputs],
        flops=flops // 3,
    )
    partial = call(
        functools.partial(kgrad_kernel, ksize),
        [sds((packed, packed), BF)],
        [shifted, own_part, hidden_near, hidden_far],
        [pltpu.VMEM((3, rows * packed // LANES, mix, LANES), F32)],
        flops * 2 // 3,
    )[0]
    total = reduce_all(partial)

    back = call(
        functools.partial(conv_kernel, ksize),
        [sds((rows, channels, width), BF)],
        [taps, grad, grad_near, grad_far],
        scratch,
        2 * n * n * rows * lanes,
    )[0]
    grad_hidden = jnp.transpose(back, (1, 0, 2))[None]

    norm = 1.0 / float(members * rows_total * width) ** 0.5
    grad_kernel = call(
        functools.partial(final_kernel, ksize, channels, norm),
        [sds((ksize, ksize, channels, channels), F32)],
        [total],
        [
            pltpu.VMEM((ksize, ksize, channels, channels), F32),
            pltpu.SemaphoreType.DMA((ksize,)),
        ],
        outside=True,
    )[0]
    return (grad_hidden, grad_kernel)


def solution(mesh):
    space, members = mesh.devices.shape
    fine = Mesh(
        mesh.devices.reshape(space, members // 2, 2), ("space", "chip", "core")
    )
    member = ("chip", "core")

    return jax.shard_map(
        body,
        mesh=fine,
        in_specs=(
            P(member, None, "space", None),
            P(None, ("space", *member)),
            P(),
            P(member, None, "space", None),
            P(),
        ),
        out_specs=(P(member, None, "space", None), P()),
        check_vma=False,
    )
```

```python
import functools
import math

import jax
import jax.numpy as jnp
import numpy as np
from jax import lax
from jax.experimental import pallas as pl
from jax.experimental.pallas import tpu as pltpu
from jax.sharding import Mesh, PartitionSpec as P


smoothing = 1.0
LANES = 128
BF = jnp.bfloat16
F32 = jnp.float32
VM = pl.BlockSpec(memory_space=pltpu.VMEM)
ANY = pl.BlockSpec(memory_space=pltpu.HBM)


def up(n, k):
    return -(-n // k) * k


def area_weights(rows_total):
    index = np.arange(rows_total)
    latitude = (index + 0.5) * (np.pi / rows_total) - np.pi / 2
    cosine = np.cos(latitude)
    return cosine / np.mean(cosine)


def call(kernel, outs, ins, scratch=(), flops=0, anywhere=(), outside=False, spare=3 << 20):
    nbytes = sum(x.size * x.dtype.itemsize for x in (*ins, *outs))
    held = sum(
        up(s.shape[-1], LANES) * math.prod(s.shape[:-1]) * s.dtype.itemsize
        for s in scratch
        if s.memory_space == pltpu.VMEM
    )
    return pl.pallas_call(
        kernel,
        out_shape=list(outs),
        in_specs=[ANY if i in anywhere else VM for i in range(len(ins))],
        out_specs=[ANY if outside else VM for _ in outs],
        scratch_shapes=list(scratch),
        cost_estimate=pl.CostEstimate(
            flops=flops, bytes_accessed=nbytes, transcendentals=0
        ),
        compiler_params=pltpu.CompilerParams(vmem_limit_bytes=held + spare),
    )(*ins)


def lane_iota(shape):
    return lax.broadcasted_iota(jnp.int32, shape, len(shape) - 1)


def mixed(ref):
    x = ref[0]
    return x.reshape(x.shape[0] * x.shape[1], x.shape[2])


def own_kernel(s_ref, x_ref, scale_ref, own_ref, s_scr, x_scr, sem):
    copies = [
        pltpu.make_async_copy(s_ref, s_scr, sem.at[0]),
        pltpu.make_async_copy(x_ref, x_scr, sem.at[1]),
    ]
    for copy in copies:
        copy.start()
    copies[0].wait()
    n, c = scale_ref.shape[0], s_ref.shape[1]
    i = lax.broadcasted_iota(jnp.int32, (n, c), 0)
    j = lax.broadcasted_iota(jnp.int32, (n, c), 1)
    s = jnp.broadcast_to(s_scr[...], (n, c))
    s = jnp.sum(jnp.where(i // (n // c) == j, s, 0.0), axis=1, keepdims=True)
    scale_ref[...] = jnp.broadcast_to(s * s, scale_ref.shape)
    copies[1].wait()
    own_ref[...] = mixed(x_scr)


def pick(table, index):
    out = jnp.float32(table[0])
    for i, v in enumerate(table[1:], 1):
        out = jnp.where(index == i, jnp.float32(v), out)
    return out


def sums(x, rows):
    x = jnp.sum(x, axis=0)
    step = rows
    while step < 8:
        x = x + pltpu.roll(x, step, 0)
        step *= 2
    return x


def tiles(width):
    return [(low, min(low + LANES, width)) for low in range(0, width, LANES)]


def blocks(x):
    return x.reshape(x.shape[0] // 8, 8, x.shape[1])


def pair_kernel(rows, s_ref, own_ref, *refs):
    *others, o_ref, mix_scr = refs
    for d, other in enumerate(others):
        mix_scr[d] = mixed(other)
    for low, high in tiles(mix_scr.shape[2]):
        sq = blocks(s_ref[:, : high - low])
        own = blocks(own_ref[:, low:high].astype(F32))
        self_inverse = 1.0 / jnp.sqrt(smoothing)
        total = jnp.full(own.shape[1:], self_inverse, F32)
        mixture = own * self_inverse
        for d in range(len(others)):
            other = blocks(mix_scr[d, :, low:high].astype(F32))
            diff = own - other
            inverse = lax.rsqrt(sums(diff * diff * sq, rows) + smoothing)
            total = total + inverse
            mixture = mixture + other * inverse[None]
        o_ref[:, low:high] = (own * total[None] - mixture).reshape(-1, high - low)


def energy_kernel(span, members, weights, s_ref, own_ref, pair_ref, *refs):
    truths = refs[:members]
    o_ref, part_scr, truth, grad, sem = refs[members:]
    rows, channels, lanes = o_ref.shape
    width = own_ref.shape[1]
    mix = channels * rows
    parts = members // rows
    me = lax.axis_index("chip") * 2 + lax.axis_index("core")
    first = lax.axis_index("space") * rows
    copies = [
        pltpu.make_async_copy(truths[d], part_scr.at[me ^ d], sem.at[d])
        for d in range(members)
    ]
    for copy in copies:
        copy.start()
    i = lax.broadcasted_iota(jnp.int32, (mix, channels), 0)
    j = lax.broadcasted_iota(jnp.int32, (mix, channels), 1)
    place = [(i == j * rows + r).astype(BF) for r in range(rows)]
    for copy in copies:
        copy.wait()
    for k in range(parts):
        truth[:, k * span : (k + 1) * span] = sum(
            jnp.dot(place[r], part_scr[r * parts + k], preferred_element_type=F32)
            for r in range(rows)
        )
    sub = lax.broadcasted_iota(jnp.int32, (8, LANES), 0) % rows
    pattern = jnp.full((8, LANES), pick(weights, first), F32)
    for r in range(1, rows):
        pattern = jnp.where(sub == r, pick(weights, first + r), pattern)
    grad[width // LANES] = jnp.zeros((mix, LANES), F32)
    for low, high in tiles(width):
        n = high - low
        sq = blocks(s_ref[:, :n])
        own = blocks(own_ref[:, low:high].astype(F32))
        offset = own - blocks(truth[:, low:high])
        direct = lax.rsqrt(sums(offset * offset * sq, rows) + smoothing)
        g = offset * direct[None] - blocks(pair_ref[:, low:high]) * (1.0 / members)
        g = g * (sq * pattern[None, :, :n])
        grad[low // LANES, :, :n] = g.reshape(mix, n)
    last = width // LANES
    body, head = grad[last], grad[0]
    lane = lane_iota(body.shape)
    off = width - last * LANES
    wrapped = jnp.where(
        (lane >= off) & (lane < off + 2), pltpu.roll(head, off, 1), body
    )
    tail = pltpu.roll(body, LANES - off, 1)
    grad[last] = jnp.where(lane >= LANES - 2, tail, wrapped)
    for r in range(rows):
        for tile in range(lanes // LANES):
            g = grad[tile, pl.ds(r, channels, stride=rows), :]
            o_ref[r, :, tile * LANES : (tile + 1) * LANES] = g.astype(BF)


def over_lanes(h, shifted):
    rows, n, _ = shifted.shape
    s = shifted[...].reshape(rows * n, shifted.shape[2])[:, : h.shape[1]]
    return lax.dot_general(h, s, (((1,), (1,)), ((), ())), preferred_element_type=F32)


def kgrad_own_kernel(ksize, g_ref, own_ref, shift_ref, o_ref):
    rows, channels, lanes = g_ref.shape
    mid = ksize // 2
    for r in range(rows):
        g = g_ref[r].astype(F32)
        for b in range(ksize):
            moved = g if b == mid else pltpu.roll(g, (mid - b) % lanes, 1)
            shift_ref[r, b * channels : (b + 1) * channels] = moved.astype(BF)
        rest = shift_ref.shape[1] - ksize * channels
        shift_ref[r, ksize * channels :] = jnp.zeros((rest, lanes), BF)
    o_ref[...] = over_lanes(mixed(own_ref), shift_ref)


def kgrad_kernel(ksize, shift_ref, own_ref, near_ref, far_ref, o_ref, acc):
    channels, rows = near_ref.shape[1:3]
    n = shift_ref.shape[1]
    odd = lax.axis_index("space") % 2
    mix = rows * channels
    both = over_lanes(
        jnp.concatenate([mixed(near_ref), mixed(far_ref)], axis=0), shift_ref
    )
    near, far = 2 * (1 - odd), 2 * odd
    for t in range(acc.shape[1]):
        lanes = slice(t * LANES, (t + 1) * LANES)
        acc[1, t] = own_ref[:, lanes]
        acc[near, t] = both[:mix, lanes]
        acc[far, t] = both[mix:, lanes]
    for i in range(ksize):
        for t in range(n // LANES):
            tap = None
            for r in range(rows):
                band, row = divmod(rows - ksize // 2 + r + i, rows)
                part = acc[
                    band, r * (n // LANES) + t, pl.ds(row, channels, stride=rows), :
                ]
                tap = part if tap is None else tap + part
            o_ref[
                i * channels : (i + 1) * channels, t * LANES : (t + 1) * LANES
            ] = tap.astype(o_ref.dtype)
    used = ksize * channels
    o_ref[used:] = jnp.zeros((o_ref.shape[0] - used, n), o_ref.dtype)


def gather_rows(own, near, far, scr):
    rows = scr.shape[0] // 3
    odd = lax.axis_index("space") % 2
    above, below = 2 * rows * (1 - odd), 2 * rows * odd
    for r in range(rows):
        scr[rows + r] = own(r)
        scr[above + r] = near(r)
        scr[below + r] = far(r)


def conv_kernel(ksize, w_ref, own_ref, near_ref, far_ref, o_ref, g_scr):
    rows, channels, lanes = own_ref.shape
    width = o_ref.shape[2]
    mid = ksize // 2
    gather_rows(
        lambda r: own_ref[r], lambda r: near_ref[r], lambda r: far_ref[r], g_scr
    )
    w = w_ref[...]
    for r in range(rows):
        g = g_scr[r : r + ksize].reshape(ksize * channels, lanes)
        y = jnp.dot(w, g, preferred_element_type=F32)
        out = None
        for b in range(ksize):
            part = y[b * channels : (b + 1) * channels]
            if b != mid:
                part = pltpu.roll(part, (mid - b) % lanes, 1)
            out = part if out is None else out + part
        o_ref[r] = out[:, :width].astype(o_ref.dtype)


def final_kernel(ksize, channels, norm, x_ref, o_ref, scr, sem):
    copies = []
    for a in range(ksize):
        i = (ksize - 1 - a) * channels
        for b in range(ksize):
            j = b * channels
            scr[a, b] = x_ref[i : i + channels, j : j + channels].astype(F32) * norm
        copies.append(pltpu.make_async_copy(scr.at[a], o_ref.at[a], sem.at[a]))
        copies[-1].start()
    for copy in copies:
        copy.wait()


def flip(x, axis, bit):
    size = lax.axis_size(axis)
    return lax.ppermute(x, axis, [(i, i ^ bit) for i in range(size)])


def along(x):
    size = lax.axis_size("space")
    pairs = [(i, i + 2) for i in range(0, size - 2, 2)]
    pairs += [(i, i - 2) for i in range(3, size, 2)]
    return lax.ppermute(x, "space", pairs)


def across(x):
    size = lax.axis_size("space")
    pairs = [(i, i + 1) for i in range(1, size - 1, 2)]
    pairs += [(i, i - 1) for i in range(2, size, 2)]
    return lax.ppermute(x, "space", pairs)


def bits(axis):
    size, out = lax.axis_size(axis), []
    while (1 << len(out)) < size:
        out.append(1 << len(out))
    return out


def add(a, b):
    return (a.astype(F32) + b.astype(F32)).astype(BF)


def own_bit(axis, bit):
    return (lax.axis_index(axis) // bit) & 1


def halve(x, axis, bit):
    high = own_bit(axis, bit)
    n = x.shape[0] // 2
    keep = lax.dynamic_slice_in_dim(x, high * n, n, 0)
    give = lax.dynamic_slice_in_dim(x, (1 - high) * n, n, 0)
    return add(keep, flip(give, axis, bit))


def join(x, axis, bit):
    other = flip(x, axis, bit)
    both = jnp.concatenate([x, other], axis=0)
    swapped = jnp.concatenate([other, x], axis=0)
    return jnp.where(own_bit(axis, bit) == 0, both, swapped)


def reduce_all(x):
    core, first = ("core", 1), ("space", 2)
    x = halve(x, *core)
    x = halve(x, *first)
    rest = [("space", b) for b in bits("space")[2:]]
    rest += [("chip", b) for b in bits("chip")] + [("space", 1)]
    for axis in rest:
        x = add(x, flip(x, *axis))
    x = join(x, *first)
    return join(x, *core)


def body(prediction_maps, truth_analysis, reciprocal_spread, deconv_inputs, filter_tensor):
    channels, rows, width = prediction_maps.shape[1:]
    ksize = filter_tensor.shape[0]
    members = lax.axis_size("chip") * lax.axis_size("core")
    rows_total = rows * lax.axis_size("space")
    lanes = up(width + 4, LANES)
    span = truth_analysis.shape[1]
    sds = jax.ShapeDtypeStruct
    slab = sds((rows, channels, lanes), BF)
    scratch = [pltpu.VMEM((3 * rows, channels, lanes), BF)]

    def core(x):
        return flip(x, "core", 1)

    def spread(x):
        have = [x]
        for bit in bits("chip"):
            have += [flip(h, "chip", bit) for h in have]
        return have

    fields = spread(prediction_maps)
    near = flip(deconv_inputs, "space", 1)
    far = across(deconv_inputs)
    truth = truth_analysis.astype(BF)
    truths = spread(truth)
    mix = rows * channels
    scale, own = call(
        own_kernel,
        [sds((mix, LANES), F32), sds((mix, width), BF)],
        [reciprocal_spread[None], prediction_maps],
        [
            pltpu.VMEM((1, channels), F32),
            pltpu.VMEM((1, channels, rows, width), BF),
            pltpu.SemaphoreType.DMA((2,)),
        ],
        anywhere=[0, 1],
    )
    taps = jnp.transpose(filter_tensor, (1, 2, 0, 3)).reshape(
        ksize * channels, ksize * channels
    )
    arrived, seen = [], []
    for i, (x, t) in enumerate(zip(fields, truths)):
        arrived += [x, core(x)] if i else [core(x)]
        seen += [t, core(t)]

    table = [float(v) for v in area_weights(rows_total)]
    paired = call(
        functools.partial(pair_kernel, rows),
        [sds((mix, width), F32)],
        [scale, own, *arrived],
        [pltpu.VMEM((members - 1, mix, width), BF)],
        spare=max(3, members) << 20,
    )[0]
    grad = call(
        functools.partial(energy_kernel, span, members, table),
        [slab],
        [scale, own, paired, *seen],
        [
            pltpu.VMEM((members, channels, span), BF),
            pltpu.VMEM((mix, lanes), F32),
            pltpu.VMEM((lanes // LANES, mix, LANES), F32),
            pltpu.SemaphoreType.DMA((members,)),
        ],
        anywhere=range(3, 3 + members),
    )[0]

    grad_near = flip(grad, "space", 1)
    grad_far = along(grad_near)

    n = ksize * channels
    packed = up(n, LANES)
    flops = 2 * n * n * rows * lanes
    shifted, own_part = call(
        functools.partial(kgrad_own_kernel, ksize),
        [sds((rows, packed, lanes), BF), sds((mix, rows * packed), F32)],
        [grad, deconv_inputs],
        flops=flops // 3,
    )
    partial = call(
        functools.partial(kgrad_kernel, ksize),
        [sds((packed, packed), BF)],
        [shifted, own_part, near, far],
        [pltpu.VMEM((3, rows * packed // LANES, mix, LANES), F32)],
        flops * 2 // 3,
    )[0]
    total = reduce_all(partial)

    back = call(
        functools.partial(conv_kernel, ksize),
        [sds((rows, channels, width), BF)],
        [taps, grad, grad_near, grad_far],
        scratch,
        2 * n * n * rows * lanes,
    )[0]
    grad_hidden = jnp.transpose(back, (1, 0, 2))[None]

    norm = 1.0 / float(members * rows_total * width) ** 0.5
    grad_kernel = call(
        functools.partial(final_kernel, ksize, channels, norm),
        [sds((ksize, ksize, channels, channels), F32)],
        [total],
        [
            pltpu.VMEM((ksize, ksize, channels, channels), F32),
            pltpu.SemaphoreType.DMA((ksize,)),
        ],
        outside=True,
    )[0]
    return (grad_hidden, grad_kernel)


def solution(mesh):
    space, members = mesh.devices.shape
    fine = Mesh(
        mesh.devices.reshape(space, members // 2, 2), ("space", "chip", "core")
    )
    member = ("chip", "core")

    return jax.shard_map(
        body,
        mesh=fine,
        in_specs=(
            P(member, None, "space", None),
            P(None, ("space", *member)),
            P(),
            P(member, None, "space", None),
            P(),
        ),
        out_specs=(P(member, None, "space", None), P()),
        check_vma=False,
    )
```

```python
import functools
import math

import jax
import jax.numpy as jnp
import numpy as np
from jax import lax
from jax.experimental import pallas as pl
from jax.experimental.pallas import tpu as pltpu
from jax.sharding import Mesh, PartitionSpec as P


smoothing = 1.0
LANES = 128
BF = jnp.bfloat16
F32 = jnp.float32
VM = pl.BlockSpec(memory_space=pltpu.VMEM)
ANY = pl.BlockSpec(memory_space=pltpu.HBM)


def up(n, k):
    return -(-n // k) * k


def area_weights(rows_total):
    index = np.arange(rows_total)
    latitude = (index + 0.5) * (np.pi / rows_total) - np.pi / 2
    cosine = np.cos(latitude)
    return cosine / np.mean(cosine)


def call(kernel, outs, ins, scratch=(), flops=0, anywhere=(), outside=False, aliases={}, spare=3 << 20):
    nbytes = sum(x.size * x.dtype.itemsize for x in (*ins, *outs))
    held = sum(
        up(s.shape[-1], LANES) * math.prod(s.shape[:-1]) * s.dtype.itemsize
        for s in scratch
        if s.memory_space == pltpu.VMEM
    )
    return pl.pallas_call(
        kernel,
        out_shape=list(outs),
        in_specs=[ANY if i in anywhere else VM for i in range(len(ins))],
        out_specs=[ANY if outside else VM for _ in outs],
        scratch_shapes=list(scratch),
        input_output_aliases=aliases,
        cost_estimate=pl.CostEstimate(
            flops=flops, bytes_accessed=nbytes, transcendentals=0
        ),
        compiler_params=pltpu.CompilerParams(vmem_limit_bytes=held + spare),
    )(*ins)


def lane_iota(shape):
    return lax.broadcasted_iota(jnp.int32, shape, len(shape) - 1)


def mixed(ref):
    x = ref[0]
    return x.reshape(x.shape[0] * x.shape[1], x.shape[2])


def own_kernel(s_ref, x_ref, scale_ref, own_ref, s_scr, x_scr, sem):
    copies = [
        pltpu.make_async_copy(s_ref, s_scr, sem.at[0]),
        pltpu.make_async_copy(x_ref, x_scr, sem.at[1]),
    ]
    for copy in copies:
        copy.start()
    copies[0].wait()
    n, c = scale_ref.shape[0], s_ref.shape[1]
    i = lax.broadcasted_iota(jnp.int32, (n, c), 0)
    j = lax.broadcasted_iota(jnp.int32, (n, c), 1)
    s = jnp.broadcast_to(s_scr[...], (n, c))
    s = jnp.sum(jnp.where(i // (n // c) == j, s, 0.0), axis=1, keepdims=True)
    scale_ref[...] = jnp.broadcast_to(s * s, scale_ref.shape)
    copies[1].wait()
    own_ref[...] = mixed(x_scr)


def pick(table, index):
    out = jnp.float32(table[0])
    for i, v in enumerate(table[1:], 1):
        out = jnp.where(index == i, jnp.float32(v), out)
    return out


def sums(x, rows):
    x = jnp.sum(x, axis=0)
    step = rows
    while step < 8:
        x = x + pltpu.roll(x, step, 0)
        step *= 2
    return x


def tiles(width):
    return [(low, min(low + LANES, width)) for low in range(0, width, LANES)]


def blocks(x):
    return x.reshape(x.shape[0] // 8, 8, x.shape[1])


def pair_kernel(rows, s_ref, own_ref, *refs):
    *others, o_ref, mix_scr = refs
    for d, other in enumerate(others):
        mix_scr[d] = mixed(other)
    for low, high in tiles(mix_scr.shape[2]):
        sq = blocks(s_ref[:, : high - low])
        own = blocks(own_ref[:, low:high].astype(F32))
        self_inverse = 1.0 / jnp.sqrt(smoothing)
        total = jnp.full(own.shape[1:], self_inverse, F32)
        mixture = own * self_inverse
        for d in range(len(others)):
            other = blocks(mix_scr[d, :, low:high].astype(F32))
            diff = own - other
            inverse = lax.rsqrt(sums(diff * diff * sq, rows) + smoothing)
            total = total + inverse
            mixture = mixture + other * inverse[None]
        o_ref[:, low:high] = (own * total[None] - mixture).reshape(-1, high - low)


def energy_kernel(span, members, weights, s_ref, own_ref, pair_ref, *refs):
    truths = refs[:members]
    o_ref, part_scr, truth, grad, sem = refs[members:]
    rows, channels, lanes = o_ref.shape
    width = own_ref.shape[1]
    mix = channels * rows
    parts = members // rows
    me = lax.axis_index("chip") * 2 + lax.axis_index("core")
    first = lax.axis_index("space") * rows
    copies = [
        pltpu.make_async_copy(truths[d], part_scr.at[me ^ d], sem.at[d])
        for d in range(members)
    ]
    for copy in copies:
        copy.start()
    i = lax.broadcasted_iota(jnp.int32, (mix, channels), 0)
    j = lax.broadcasted_iota(jnp.int32, (mix, channels), 1)
    place = [(i == j * rows + r).astype(BF) for r in range(rows)]
    for copy in copies:
        copy.wait()
    for k in range(parts):
        truth[:, k * span : (k + 1) * span] = sum(
            jnp.dot(place[r], part_scr[r * parts + k], preferred_element_type=F32)
            for r in range(rows)
        )
    sub = lax.broadcasted_iota(jnp.int32, (8, LANES), 0) % rows
    pattern = jnp.full((8, LANES), pick(weights, first), F32)
    for r in range(1, rows):
        pattern = jnp.where(sub == r, pick(weights, first + r), pattern)
    grad[width // LANES] = jnp.zeros((mix, LANES), F32)
    for low, high in tiles(width):
        n = high - low
        sq = blocks(s_ref[:, :n])
        own = blocks(own_ref[:, low:high].astype(F32))
        offset = own - blocks(truth[:, low:high])
        direct = lax.rsqrt(sums(offset * offset * sq, rows) + smoothing)
        g = offset * direct[None] - blocks(pair_ref[:, low:high]) * (1.0 / members)
        g = g * (sq * pattern[None, :, :n])
        grad[low // LANES, :, :n] = g.reshape(mix, n)
    last = width // LANES
    body, head = grad[last], grad[0]
    lane = lane_iota(body.shape)
    off = width - last * LANES
    wrapped = jnp.where(
        (lane >= off) & (lane < off + 2), pltpu.roll(head, off, 1), body
    )
    tail = pltpu.roll(body, LANES - off, 1)
    grad[last] = jnp.where(lane >= LANES - 2, tail, wrapped)
    for r in range(rows):
        for tile in range(lanes // LANES):
            g = grad[tile, pl.ds(r, channels, stride=rows), :]
            o_ref[r, :, tile * LANES : (tile + 1) * LANES] = g.astype(BF)


def over_lanes(h, shifted):
    rows, n, _ = shifted.shape
    s = shifted[...].reshape(rows * n, shifted.shape[2])[:, : h.shape[1]]
    return lax.dot_general(h, s, (((1,), (1,)), ((), ())), preferred_element_type=F32)


def kgrad_own_kernel(ksize, g_ref, own_ref, shift_ref, o_ref):
    rows, channels, lanes = g_ref.shape
    mid = ksize // 2
    for r in range(rows):
        g = g_ref[r].astype(F32)
        for b in range(ksize):
            moved = g if b == mid else pltpu.roll(g, (mid - b) % lanes, 1)
            shift_ref[r, b * channels : (b + 1) * channels] = moved.astype(BF)
        rest = shift_ref.shape[1] - ksize * channels
        shift_ref[r, ksize * channels :] = jnp.zeros((rest, lanes), BF)
    o_ref[...] = over_lanes(mixed(own_ref), shift_ref)


def kgrad_kernel(ksize, shift_ref, own_ref, near_ref, far_ref, o_ref, acc):
    channels, rows = near_ref.shape[1:3]
    n = shift_ref.shape[1]
    odd = lax.axis_index("space") % 2
    mix = rows * channels
    both = over_lanes(
        jnp.concatenate([mixed(near_ref), mixed(far_ref)], axis=0), shift_ref
    )
    near, far = 2 * (1 - odd), 2 * odd
    for t in range(acc.shape[1]):
        lanes = slice(t * LANES, (t + 1) * LANES)
        acc[1, t] = own_ref[:, lanes]
        acc[near, t] = both[:mix, lanes]
        acc[far, t] = both[mix:, lanes]
    for i in range(ksize):
        for t in range(n // LANES):
            tap = None
            for r in range(rows):
                band, row = divmod(rows - ksize // 2 + r + i, rows)
                part = acc[
                    band, r * (n // LANES) + t, pl.ds(row, channels, stride=rows), :
                ]
                tap = part if tap is None else tap + part
            o_ref[
                i * channels : (i + 1) * channels, t * LANES : (t + 1) * LANES
            ] = tap.astype(o_ref.dtype)
    used = ksize * channels
    o_ref[used:] = jnp.zeros((o_ref.shape[0] - used, n), o_ref.dtype)


def gather_rows(own, near, far, scr):
    rows = scr.shape[0] // 3
    odd = lax.axis_index("space") % 2
    above, below = 2 * rows * (1 - odd), 2 * rows * odd
    for r in range(rows):
        scr[rows + r] = own(r)
        scr[above + r] = near(r)
        scr[below + r] = far(r)


def conv_kernel(ksize, w_ref, own_ref, near_ref, far_ref, o_ref, g_scr, tile_scr, mix_scr):
    rows, channels, lanes = own_ref.shape
    width = o_ref.shape[3]
    mid = ksize // 2
    gather_rows(
        lambda r: own_ref[r], lambda r: near_ref[r], lambda r: far_ref[r], g_scr
    )
    w = w_ref[...]
    for r in range(rows):
        g = g_scr[r : r + ksize].reshape(ksize * channels, lanes)
        y = jnp.dot(w, g, preferred_element_type=F32)
        out = None
        for b in range(ksize):
            part = y[b * channels : (b + 1) * channels]
            if b != mid:
                part = pltpu.roll(part, (mid - b) % lanes, 1)
            out = part if out is None else out + part
        for t in range(tile_scr.shape[0]):
            row = pl.ds(r, channels, stride=rows)
            tile_scr[t, row, :] = out[:, t * LANES : (t + 1) * LANES]
    for low, high in tiles(width):
        mix_scr[:, low:high] = tile_scr[low // LANES][:, : high - low].astype(BF)
    o_ref[0] = mix_scr[...].reshape(channels, rows, width)


def final_kernel(ksize, channels, norm, own, x_ref, *refs):
    o_ref, scr, sem = refs[-3:]
    n = x_ref.shape[0]
    half = lax.axis_index("core") % 2
    half = half if own else 1 - half
    for h in range(2):

        @pl.when(half == h)
        def _():
            copies = []
            for i in range(ksize):
                low = max(i * channels, h * n)
                high = min((i + 1) * channels, (h + 1) * n)
                if low >= high:
                    continue
                a, rows = ksize - 1 - i, slice(low - i * channels, high - i * channels)
                for b in range(ksize):
                    x = x_ref[low - h * n : high - h * n, b * channels : (b + 1) * channels]
                    scr[a, b, rows] = x.astype(F32) * norm
                at = (a, slice(None), pl.ds(rows.start, high - low))
                copies.append(
                    pltpu.make_async_copy(scr.at[at], o_ref.at[at], sem.at[a])
                )
                copies[-1].start()
            for copy in copies:
                copy.wait()


def flip(x, axis, bit):
    size = lax.axis_size(axis)
    return lax.ppermute(x, axis, [(i, i ^ bit) for i in range(size)])


def along(x):
    size = lax.axis_size("space")
    pairs = [(i, i + 2) for i in range(0, size - 2, 2)]
    pairs += [(i, i - 2) for i in range(3, size, 2)]
    return lax.ppermute(x, "space", pairs)


def across(x):
    size = lax.axis_size("space")
    pairs = [(i, i + 1) for i in range(1, size - 1, 2)]
    pairs += [(i, i - 1) for i in range(2, size, 2)]
    return lax.ppermute(x, "space", pairs)


def bits(axis):
    size, out = lax.axis_size(axis), []
    while (1 << len(out)) < size:
        out.append(1 << len(out))
    return out


def add(a, b):
    return (a.astype(F32) + b.astype(F32)).astype(BF)


def own_bit(axis, bit):
    return (lax.axis_index(axis) // bit) & 1


def halve(x, axis, bit):
    high = own_bit(axis, bit)
    n = x.shape[0] // 2
    keep = lax.dynamic_slice_in_dim(x, high * n, n, 0)
    give = lax.dynamic_slice_in_dim(x, (1 - high) * n, n, 0)
    return add(keep, flip(give, axis, bit))


def join(x, axis, bit):
    other = flip(x, axis, bit)
    both = jnp.concatenate([x, other], axis=0)
    swapped = jnp.concatenate([other, x], axis=0)
    return jnp.where(own_bit(axis, bit) == 0, both, swapped)


def reduce_all(x):
    core, first = ("core", 1), ("space", 2)
    x = halve(x, *core)
    x = halve(x, *first)
    rest = [("space", b) for b in bits("space")[2:]]
    rest += [("chip", b) for b in bits("chip")] + [("space", 1)]
    for axis in rest:
        x = add(x, flip(x, *axis))
    x = join(x, *first)
    return x, flip(x, *core)


def body(prediction_maps, truth_analysis, reciprocal_spread, deconv_inputs, filter_tensor):
    channels, rows, width = prediction_maps.shape[1:]
    ksize = filter_tensor.shape[0]
    members = lax.axis_size("chip") * lax.axis_size("core")
    rows_total = rows * lax.axis_size("space")
    lanes = up(width + 4, LANES)
    span = truth_analysis.shape[1]
    sds = jax.ShapeDtypeStruct
    slab = sds((rows, channels, lanes), BF)

    def core(x):
        return flip(x, "core", 1)

    def spread(x):
        have = [x]
        for bit in bits("chip"):
            have += [flip(h, "chip", bit) for h in have]
        return have

    fields = spread(prediction_maps)
    near = flip(deconv_inputs, "space", 1)
    far = across(deconv_inputs)
    truth = truth_analysis.astype(BF)
    truths = spread(truth)
    mix = rows * channels
    scale, own = call(
        own_kernel,
        [sds((mix, LANES), F32), sds((mix, width), BF)],
        [reciprocal_spread[None], prediction_maps],
        [
            pltpu.VMEM((1, channels), F32),
            pltpu.VMEM((1, channels, rows, width), BF),
            pltpu.SemaphoreType.DMA((2,)),
        ],
        anywhere=[0, 1],
    )
    taps = jnp.transpose(filter_tensor, (1, 2, 0, 3)).reshape(ksize * channels, ksize * channels)
    arrived, seen = [], []
    for i, (x, t) in enumerate(zip(fields, truths)):
        arrived += [x, core(x)] if i else [core(x)]
        seen += [t, core(t)]

    table = [float(v) for v in area_weights(rows_total)]
    paired = call(
        functools.partial(pair_kernel, rows),
        [sds((mix, width), F32)],
        [scale, own, *arrived],
        [pltpu.VMEM((members - 1, mix, width), BF)],
        spare=max(3, members) << 20,
    )[0]
    grad = call(
        functools.partial(energy_kernel, span, members, table),
        [slab],
        [scale, own, paired, *seen],
        [
            pltpu.VMEM((members, channels, span), BF),
            pltpu.VMEM((mix, lanes), F32),
            pltpu.VMEM((lanes // LANES, mix, LANES), F32),
            pltpu.SemaphoreType.DMA((members,)),
        ],
        anywhere=range(3, 3 + members),
    )[0]

    grad_near = flip(grad, "space", 1)
    grad_far = along(grad_near)

    n = ksize * channels
    packed = up(n, LANES)
    flops = 2 * n * n * rows * lanes
    shifted, own_part = call(
        functools.partial(kgrad_own_kernel, ksize),
        [sds((rows, packed, lanes), BF), sds((mix, rows * packed), F32)],
        [grad, deconv_inputs],
        flops=flops // 3,
    )
    partial = call(
        functools.partial(kgrad_kernel, ksize),
        [sds((packed, packed), BF)],
        [shifted, own_part, near, far],
        [pltpu.VMEM((3, rows * packed // LANES, mix, LANES), F32)],
        flops * 2 // 3,
    )[0]
    own_half, other_half = reduce_all(partial)

    grad_hidden = call(
        functools.partial(conv_kernel, ksize),
        [sds(prediction_maps.shape, BF)],
        [taps, grad, grad_near, grad_far],
        [
            pltpu.VMEM((3 * rows, channels, lanes), BF),
            pltpu.VMEM((lanes // LANES, mix, LANES), F32),
            pltpu.VMEM((mix, width), BF),
        ],
        2 * n * n * rows * lanes,
    )[0]

    norm = 1.0 / float(members * rows_total * width) ** 0.5
    shape = (ksize, ksize, channels, channels)

    def finish(own, *xs):
        return call(
            functools.partial(final_kernel, ksize, channels, norm, own),
            [sds(shape, F32)],
            xs,
            [pltpu.VMEM(shape, F32), pltpu.SemaphoreType.DMA((ksize,))],
            anywhere=[1],
            outside=True,
            aliases={} if own else {1: 0},
        )[0]

    grad_kernel = finish(True, own_half)
    grad_kernel = finish(False, other_half, grad_kernel)
    return (grad_hidden, grad_kernel)


def solution(mesh):
    space, members = mesh.devices.shape
    fine = Mesh(
        mesh.devices.reshape(space, members // 2, 2), ("space", "chip", "core")
    )
    member = ("chip", "core")

    return jax.shard_map(
        body,
        mesh=fine,
        in_specs=(
            P(member, None, "space", None),
            P(None, ("space", *member)),
            P(),
            P(member, None, "space", None),
            P(),
        ),
        out_specs=(P(member, None, "space", None), P()),
        check_vma=False,
    )
```

```python
import functools
import math

import jax
import jax.numpy as jnp
import numpy as np
from jax import lax
from jax.experimental import pallas as pl
from jax.experimental.pallas import tpu as pltpu
from jax.sharding import Mesh, PartitionSpec as P


smoothing = 1.0
LANES = 128
BF = jnp.bfloat16
F32 = jnp.float32
VM = pl.BlockSpec(memory_space=pltpu.VMEM)
ANY = pl.BlockSpec(memory_space=pltpu.HBM)


def up(n, k):
    return -(-n // k) * k


def area_weights(rows_total):
    index = np.arange(rows_total)
    latitude = (index + 0.5) * (np.pi / rows_total) - np.pi / 2
    cosine = np.cos(latitude)
    return cosine / np.mean(cosine)


def call(kernel, outs, ins, scratch=(), flops=0, anywhere=(), outside=False, aliases={}, spare=3 << 20):
    nbytes = sum(x.size * x.dtype.itemsize for x in (*ins, *outs))
    held = sum(
        up(s.shape[-1], LANES) * math.prod(s.shape[:-1]) * s.dtype.itemsize
        for s in scratch
        if s.memory_space == pltpu.VMEM
    )
    return pl.pallas_call(
        kernel,
        out_shape=list(outs),
        in_specs=[ANY if i in anywhere else VM for i in range(len(ins))],
        out_specs=[ANY if outside else VM for _ in outs],
        scratch_shapes=list(scratch),
        input_output_aliases=aliases,
        cost_estimate=pl.CostEstimate(
            flops=flops, bytes_accessed=nbytes, transcendentals=0
        ),
        compiler_params=pltpu.CompilerParams(vmem_limit_bytes=held + spare),
    )(*ins)


def lane_iota(shape):
    return lax.broadcasted_iota(jnp.int32, shape, len(shape) - 1)


def mixed(ref):
    x = ref[0]
    return x.reshape(x.shape[0] * x.shape[1], x.shape[2])


def own_kernel(s_ref, x_ref, scale_ref, own_ref, s_scr, x_scr, sem):
    copies = [
        pltpu.make_async_copy(s_ref, s_scr, sem.at[0]),
        pltpu.make_async_copy(x_ref, x_scr, sem.at[1]),
    ]
    for copy in copies:
        copy.start()
    copies[0].wait()
    n, c = scale_ref.shape[0], s_ref.shape[1]
    i = lax.broadcasted_iota(jnp.int32, (n, c), 0)
    j = lax.broadcasted_iota(jnp.int32, (n, c), 1)
    s = jnp.broadcast_to(s_scr[...], (n, c))
    s = jnp.sum(jnp.where(i // (n // c) == j, s, 0.0), axis=1, keepdims=True)
    scale_ref[...] = jnp.broadcast_to(s * s, scale_ref.shape)
    copies[1].wait()
    own_ref[...] = mixed(x_scr)


def pick(table, index):
    out = jnp.float32(table[0])
    for i, v in enumerate(table[1:], 1):
        out = jnp.where(index == i, jnp.float32(v), out)
    return out


def sums(x, rows):
    x = jnp.sum(x, axis=0)
    step = rows
    while step < 8:
        x = x + pltpu.roll(x, step, 0)
        step *= 2
    return x


def tiles(width):
    return [(low, min(low + LANES, width)) for low in range(0, width, LANES)]


def blocks(x):
    return x.reshape(x.shape[0] // 8, 8, x.shape[1])


def pair_kernel(rows, begun, s_ref, own_ref, *refs):
    *others, o_ref, mix_scr = refs
    sum_ref = others.pop() if begun else None
    for d, other in enumerate(others):
        mix_scr[d] = mixed(other)
    for low, high in tiles(mix_scr.shape[2]):
        sq = blocks(s_ref[:, : high - low])
        own = blocks(own_ref[:, low:high].astype(F32))
        self_inverse = 0.0 if begun else 1.0 / jnp.sqrt(smoothing)
        total = jnp.full(own.shape[1:], self_inverse, F32)
        mixture = own * self_inverse
        if begun:
            mixture = mixture - blocks(sum_ref[:, low:high])
        for d in range(len(others)):
            other = blocks(mix_scr[d, :, low:high].astype(F32))
            diff = own - other
            inverse = lax.rsqrt(sums(diff * diff * sq, rows) + smoothing)
            total = total + inverse
            mixture = mixture + other * inverse[None]
        o_ref[:, low:high] = (own * total[None] - mixture).reshape(-1, high - low)


def energy_kernel(span, members, weights, s_ref, own_ref, pair_ref, *refs):
    truths = refs[:members]
    o_ref, part_scr, truth, grad, sem = refs[members:]
    rows, channels, lanes = o_ref.shape
    width = own_ref.shape[1]
    mix = channels * rows
    parts = members // rows
    me = lax.axis_index("chip") * 2 + lax.axis_index("core")
    first = lax.axis_index("space") * rows
    copies = [
        pltpu.make_async_copy(truths[d], part_scr.at[me ^ d], sem.at[d])
        for d in range(members)
    ]
    for copy in copies:
        copy.start()
    i = lax.broadcasted_iota(jnp.int32, (mix, channels), 0)
    j = lax.broadcasted_iota(jnp.int32, (mix, channels), 1)
    place = [(i == j * rows + r).astype(BF) for r in range(rows)]
    for copy in copies:
        copy.wait()
    for k in range(parts):
        truth[:, k * span : (k + 1) * span] = sum(
            jnp.dot(place[r], part_scr[r * parts + k], preferred_element_type=F32)
            for r in range(rows)
        )
    sub = lax.broadcasted_iota(jnp.int32, (8, LANES), 0) % rows
    pattern = jnp.full((8, LANES), pick(weights, first), F32)
    for r in range(1, rows):
        pattern = jnp.where(sub == r, pick(weights, first + r), pattern)
    grad[width // LANES] = jnp.zeros((mix, LANES), F32)
    for low, high in tiles(width):
        n = high - low
        sq = blocks(s_ref[:, :n])
        own = blocks(own_ref[:, low:high].astype(F32))
        offset = own - blocks(truth[:, low:high])
        direct = lax.rsqrt(sums(offset * offset * sq, rows) + smoothing)
        g = offset * direct[None] - blocks(pair_ref[:, low:high]) * (1.0 / members)
        g = g * (sq * pattern[None, :, :n])
        grad[low // LANES, :, :n] = g.reshape(mix, n)
    last = width // LANES
    body, head = grad[last], grad[0]
    lane = lane_iota(body.shape)
    off = width - last * LANES
    wrapped = jnp.where(
        (lane >= off) & (lane < off + 2), pltpu.roll(head, off, 1), body
    )
    tail = pltpu.roll(body, LANES - off, 1)
    grad[last] = jnp.where(lane >= LANES - 2, tail, wrapped)
    for r in range(rows):
        for tile in range(lanes // LANES):
            g = grad[tile, pl.ds(r, channels, stride=rows), :]
            o_ref[r, :, tile * LANES : (tile + 1) * LANES] = g.astype(BF)


def over_lanes(h, shifted):
    rows, n, _ = shifted.shape
    s = shifted[...].reshape(rows * n, shifted.shape[2])[:, : h.shape[1]]
    return lax.dot_general(h, s, (((1,), (1,)), ((), ())), preferred_element_type=F32)


def kgrad_own_kernel(ksize, g_ref, own_ref, shift_ref, o_ref):
    rows, channels, lanes = g_ref.shape
    mid = ksize // 2
    for r in range(rows):
        g = g_ref[r].astype(F32)
        for b in range(ksize):
            moved = g if b == mid else pltpu.roll(g, (mid - b) % lanes, 1)
            shift_ref[r, b * channels : (b + 1) * channels] = moved.astype(BF)
        rest = shift_ref.shape[1] - ksize * channels
        shift_ref[r, ksize * channels :] = jnp.zeros((rest, lanes), BF)
    o_ref[...] = over_lanes(mixed(own_ref), shift_ref)


def kgrad_kernel(ksize, shift_ref, own_ref, near_ref, far_ref, o_ref, acc):
    channels, rows = near_ref.shape[1:3]
    n = shift_ref.shape[1]
    odd = lax.axis_index("space") % 2
    mix = rows * channels
    both = over_lanes(
        jnp.concatenate([mixed(near_ref), mixed(far_ref)], axis=0), shift_ref
    )
    near, far = 2 * (1 - odd), 2 * odd
    for t in range(acc.shape[1]):
        lanes = slice(t * LANES, (t + 1) * LANES)
        acc[1, t] = own_ref[:, lanes]
        acc[near, t] = both[:mix, lanes]
        acc[far, t] = both[mix:, lanes]
    for i in range(ksize):
        for t in range(n // LANES):
            tap = None
            for r in range(rows):
                band, row = divmod(rows - ksize // 2 + r + i, rows)
                part = acc[
                    band, r * (n // LANES) + t, pl.ds(row, channels, stride=rows), :
                ]
                tap = part if tap is None else tap + part
            o_ref[
                i * channels : (i + 1) * channels, t * LANES : (t + 1) * LANES
            ] = tap.astype(o_ref.dtype)
    used = ksize * channels
    o_ref[used:] = jnp.zeros((o_ref.shape[0] - used, n), o_ref.dtype)


def gather_rows(own, near, far, scr):
    rows = scr.shape[0] // 3
    odd = lax.axis_index("space") % 2
    above, below = 2 * rows * (1 - odd), 2 * rows * odd
    for r in range(rows):
        scr[rows + r] = own(r)
        scr[above + r] = near(r)
        scr[below + r] = far(r)


def conv_kernel(ksize, w_ref, own_ref, near_ref, far_ref, o_ref, g_scr, tile_scr, mix_scr):
    rows, channels, lanes = own_ref.shape
    width = o_ref.shape[3]
    mid = ksize // 2
    gather_rows(
        lambda r: own_ref[r], lambda r: near_ref[r], lambda r: far_ref[r], g_scr
    )
    w = w_ref[...]
    for r in range(rows):
        g = g_scr[r : r + ksize].reshape(ksize * channels, lanes)
        y = jnp.dot(w, g, preferred_element_type=F32)
        out = None
        for b in range(ksize):
            part = y[b * channels : (b + 1) * channels]
            if b != mid:
                part = pltpu.roll(part, (mid - b) % lanes, 1)
            out = part if out is None else out + part
        for t in range(tile_scr.shape[0]):
            row = pl.ds(r, channels, stride=rows)
            tile_scr[t, row, :] = out[:, t * LANES : (t + 1) * LANES]
    for low, high in tiles(width):
        mix_scr[:, low:high] = tile_scr[low // LANES][:, : high - low].astype(BF)
    o_ref[0] = mix_scr[...].reshape(channels, rows, width)


def final_kernel(ksize, channels, norm, pieces, *refs):
    xs, (o_ref, scr, sem) = refs[: len(pieces)], refs[-3:]
    core = lax.axis_index("core")
    end = lax.axis_index("space") // 2
    n = xs[0].shape[0]
    for wait in (False, True):
        for k, (other, second) in enumerate(pieces):
            quarter = 2 * ((core + other) % 2) + (end + second) % 2
            for q in range(4):

                @pl.when(quarter == q)
                def _(k=k, q=q):
                    x_ref = xs[k]
                    slot = 0
                    for i in range(ksize):
                        low = max(i * channels, q * n)
                        high = min((i + 1) * channels, (q + 1) * n)
                        if low >= high:
                            continue
                        first = low - i * channels
                        at = (ksize - 1 - i, slice(None), pl.ds(first, high - low))
                        copy = pltpu.make_async_copy(
                            scr.at[at], o_ref.at[at], sem.at[k, slot]
                        )
                        slot += 1
                        if wait:
                            copy.wait()
                            continue
                        rows = slice(first, first + high - low)
                        for b in range(ksize):
                            x = x_ref[
                                low - q * n : high - q * n,
                                b * channels : (b + 1) * channels,
                            ]
                            scr[ksize - 1 - i, b, rows] = x.astype(F32) * norm
                        copy.start()


def flip(x, axis, bit):
    size = lax.axis_size(axis)
    return lax.ppermute(x, axis, [(i, i ^ bit) for i in range(size)])


def along(x):
    size = lax.axis_size("space")
    pairs = [(i, i + 2) for i in range(0, size - 2, 2)]
    pairs += [(i, i - 2) for i in range(3, size, 2)]
    return lax.ppermute(x, "space", pairs)


def across(x):
    size = lax.axis_size("space")
    pairs = [(i, i + 1) for i in range(1, size - 1, 2)]
    pairs += [(i, i - 1) for i in range(2, size, 2)]
    return lax.ppermute(x, "space", pairs)


def bits(axis):
    size, out = lax.axis_size(axis), []
    while (1 << len(out)) < size:
        out.append(1 << len(out))
    return out


def add(a, b):
    return (a.astype(F32) + b.astype(F32)).astype(BF)


def own_bit(axis, bit):
    return (lax.axis_index(axis) // bit) & 1


def halve(x, axis, bit):
    high = own_bit(axis, bit)
    n = x.shape[0] // 2
    keep = lax.dynamic_slice_in_dim(x, high * n, n, 0)
    give = lax.dynamic_slice_in_dim(x, (1 - high) * n, n, 0)
    return add(keep, flip(give, axis, bit))


def reduce_all(x):
    core, first = ("core", 1), ("space", 2)
    x = halve(x, *core)
    x = halve(x, *first)
    rest = [("space", b) for b in bits("space")[2:]]
    rest += [("chip", b) for b in bits("chip")] + [("space", 1)]
    for axis in rest:
        x = add(x, flip(x, *axis))
    y = flip(x, *first)
    x_other = flip(x, *core)
    y_other = flip(y, *core)
    return (x, y), (x_other, y_other)


def body(prediction_maps, truth_analysis, reciprocal_spread, deconv_inputs, filter_tensor):
    channels, rows, width = prediction_maps.shape[1:]
    ksize = filter_tensor.shape[0]
    members = lax.axis_size("chip") * lax.axis_size("core")
    rows_total = rows * lax.axis_size("space")
    lanes = up(width + 4, LANES)
    span = truth_analysis.shape[1]
    sds = jax.ShapeDtypeStruct
    slab = sds((rows, channels, lanes), BF)

    def core(x):
        return flip(x, "core", 1)

    def spread(x):
        have = [x]
        for bit in bits("chip"):
            have += [flip(h, "chip", bit) for h in have]
        return have

    fields = spread(prediction_maps)
    near = flip(deconv_inputs, "space", 1)
    far = across(deconv_inputs)
    truth = truth_analysis.astype(BF)
    truths = spread(truth)
    mix = rows * channels
    scale, own = call(
        own_kernel,
        [sds((mix, LANES), F32), sds((mix, width), BF)],
        [reciprocal_spread[None], prediction_maps],
        [
            pltpu.VMEM((1, channels), F32),
            pltpu.VMEM((1, channels, rows, width), BF),
            pltpu.SemaphoreType.DMA((2,)),
        ],
        anywhere=[0, 1],
    )
    taps = jnp.transpose(filter_tensor, (1, 2, 0, 3)).reshape(
        ksize * channels, ksize * channels
    )
    arrived, seen = [], []
    for i, (x, t) in enumerate(zip(fields, truths)):
        arrived += [x, core(x)] if i else [core(x)]
        seen += [t, core(t)]

    table = [float(v) for v in area_weights(rows_total)]

    def pairs(others, so_far):
        return call(
            functools.partial(pair_kernel, rows, bool(so_far)),
            [sds((mix, width), F32)],
            [scale, own, *others, *so_far],
            [pltpu.VMEM((len(others), mix, width), BF)],
            spare=max(3, members) << 20,
        )[0]

    paired = pairs(arrived[:-1], ())
    paired = pairs(arrived[-1:], (paired,))
    grad = call(
        functools.partial(energy_kernel, span, members, table),
        [slab],
        [scale, own, paired, *seen],
        [
            pltpu.VMEM((members, channels, span), BF),
            pltpu.VMEM((mix, lanes), F32),
            pltpu.VMEM((lanes // LANES, mix, LANES), F32),
            pltpu.SemaphoreType.DMA((members,)),
        ],
        anywhere=range(3, 3 + members),
    )[0]

    grad_near = flip(grad, "space", 1)
    grad_far = along(grad_near)

    n = ksize * channels
    packed = up(n, LANES)
    flops = 2 * n * n * rows * lanes
    shifted, own_part = call(
        functools.partial(kgrad_own_kernel, ksize),
        [sds((rows, packed, lanes), BF), sds((mix, rows * packed), F32)],
        [grad, deconv_inputs],
        flops=flops // 3,
    )
    partial = call(
        functools.partial(kgrad_kernel, ksize),
        [sds((packed, packed), BF)],
        [shifted, own_part, near, far],
        [pltpu.VMEM((3, rows * packed // LANES, mix, LANES), F32)],
        flops * 2 // 3,
    )[0]
    early, late = reduce_all(partial)

    grad_hidden = call(
        functools.partial(conv_kernel, ksize),
        [sds(prediction_maps.shape, BF)],
        [taps, grad, grad_near, grad_far],
        [
            pltpu.VMEM((3 * rows, channels, lanes), BF),
            pltpu.VMEM((lanes // LANES, mix, LANES), F32),
            pltpu.VMEM((mix, width), BF),
        ],
        2 * n * n * rows * lanes,
    )[0]

    norm = 1.0 / float(members * rows_total * width) ** 0.5
    shape = (ksize, ksize, channels, channels)

    def finish(pieces, *xs):
        count = len(pieces)
        return call(
            functools.partial(final_kernel, ksize, channels, norm, pieces),
            [sds(shape, F32)],
            xs,
            [pltpu.VMEM(shape, F32), pltpu.SemaphoreType.DMA((count, 3))],
            anywhere=range(count, len(xs)),
            outside=True,
            aliases={count: 0} if len(xs) > count else {},
        )[0]

    grad_kernel = finish([(0, 0), (0, 1)], *early)
    grad_kernel = finish([(1, 0), (1, 1)], *late, grad_kernel)
    return (grad_hidden, grad_kernel)


def solution(mesh):
    space, members = mesh.devices.shape
    fine = Mesh(
        mesh.devices.reshape(space, members // 2, 2), ("space", "chip", "core")
    )
    member = ("chip", "core")

    return jax.shard_map(
        body,
        mesh=fine,
        in_specs=(
            P(member, None, "space", None),
            P(None, ("space", *member)),
            P(),
            P(member, None, "space", None),
            P(),
        ),
        out_specs=(P(member, None, "space", None), P()),
        check_vma=False,
    )
```

```python
import functools
import math

import jax
import jax.numpy as jnp
import numpy as np
from jax import lax
from jax.experimental import pallas as pl
from jax.experimental.pallas import tpu as pltpu
from jax.sharding import Mesh, PartitionSpec as P


smoothing = 1.0
LANES = 128
BF = jnp.bfloat16
F32 = jnp.float32
VM = pl.BlockSpec(memory_space=pltpu.VMEM)
ANY = pl.BlockSpec(memory_space=pltpu.HBM)


def up(n, k):
    return -(-n // k) * k


def area_weights(rows_total):
    index = np.arange(rows_total)
    latitude = (index + 0.5) * (np.pi / rows_total) - np.pi / 2
    cosine = np.cos(latitude)
    return cosine / np.mean(cosine)


def call(kernel, outs, ins, scratch=(), flops=0, anywhere=(), outside=False, aliases={}, spare=3 << 20):
    nbytes = sum(x.size * x.dtype.itemsize for x in (*ins, *outs))
    held = sum(
        up(s.shape[-1], LANES) * math.prod(s.shape[:-1]) * s.dtype.itemsize
        for s in scratch
        if s.memory_space == pltpu.VMEM
    )
    return pl.pallas_call(
        kernel,
        out_shape=list(outs),
        in_specs=[ANY if i in anywhere else VM for i in range(len(ins))],
        out_specs=[ANY if outside else VM for _ in outs],
        scratch_shapes=list(scratch),
        input_output_aliases=aliases,
        cost_estimate=pl.CostEstimate(
            flops=flops, bytes_accessed=nbytes, transcendentals=0
        ),
        compiler_params=pltpu.CompilerParams(vmem_limit_bytes=held + spare),
    )(*ins)


def lane_iota(shape):
    return lax.broadcasted_iota(jnp.int32, shape, len(shape) - 1)


def mixed(ref):
    x = ref[0]
    return x.reshape(x.shape[0] * x.shape[1], x.shape[2])


def own_kernel(s_ref, x_ref, scale_ref, own_ref, s_scr, x_scr, sem):
    copies = [
        pltpu.make_async_copy(s_ref, s_scr, sem.at[0]),
        pltpu.make_async_copy(x_ref, x_scr, sem.at[1]),
    ]
    for copy in copies:
        copy.start()
    copies[0].wait()
    n, c = scale_ref.shape[0], s_ref.shape[1]
    i = lax.broadcasted_iota(jnp.int32, (n, c), 0)
    j = lax.broadcasted_iota(jnp.int32, (n, c), 1)
    s = jnp.broadcast_to(s_scr[...], (n, c))
    s = jnp.sum(jnp.where(i // (n // c) == j, s, 0.0), axis=1, keepdims=True)
    scale_ref[...] = jnp.broadcast_to(s * s, scale_ref.shape)
    copies[1].wait()
    own_ref[...] = mixed(x_scr)


def pick(table, index):
    out = jnp.float32(table[0])
    for i, v in enumerate(table[1:], 1):
        out = jnp.where(index == i, jnp.float32(v), out)
    return out


def sums(x, rows):
    x = jnp.sum(x, axis=0)
    step = rows
    while step < 8:
        x = x + pltpu.roll(x, step, 0)
        step *= 2
    return x


def tiles(width):
    return [(low, min(low + LANES, width)) for low in range(0, width, LANES)]


def blocks(x):
    return x.reshape(x.shape[0] // 8, 8, x.shape[1])


def pair_kernel(rows, s_ref, own_ref, *refs):
    *others, o_ref, mix_scr = refs
    for d, other in enumerate(others):
        mix_scr[d] = mixed(other)
    for low, high in tiles(mix_scr.shape[2]):
        sq = blocks(s_ref[:, : high - low])
        own = blocks(own_ref[:, low:high].astype(F32))
        self_inverse = 1.0 / jnp.sqrt(smoothing)
        total = jnp.full(own.shape[1:], self_inverse, F32)
        mixture = own * self_inverse
        for d in range(len(others)):
            other = blocks(mix_scr[d, :, low:high].astype(F32))
            diff = own - other
            inverse = lax.rsqrt(sums(diff * diff * sq, rows) + smoothing)
            total = total + inverse
            mixture = mixture + other * inverse[None]
        o_ref[:, low:high] = (own * total[None] - mixture).reshape(-1, high - low)


def energy_kernel(span, members, weights, s_ref, own_ref, pair_ref, *refs):
    truths = refs[:members]
    o_ref, part_scr, truth, grad, sem = refs[members:]
    rows, channels, lanes = o_ref.shape
    width = own_ref.shape[1]
    mix = channels * rows
    parts = members // rows
    me = lax.axis_index("chip") * 2 + lax.axis_index("core")
    first = lax.axis_index("space") * rows
    copies = [
        pltpu.make_async_copy(truths[d], part_scr.at[me ^ d], sem.at[d])
        for d in range(members)
    ]
    for copy in copies:
        copy.start()
    i = lax.broadcasted_iota(jnp.int32, (mix, channels), 0)
    j = lax.broadcasted_iota(jnp.int32, (mix, channels), 1)
    place = [(i == j * rows + r).astype(BF) for r in range(rows)]
    for copy in copies:
        copy.wait()
    for k in range(parts):
        truth[:, k * span : (k + 1) * span] = sum(
            jnp.dot(place[r], part_scr[r * parts + k], preferred_element_type=F32)
            for r in range(rows)
        )
    sub = lax.broadcasted_iota(jnp.int32, (8, LANES), 0) % rows
    pattern = jnp.full((8, LANES), pick(weights, first), F32)
    for r in range(1, rows):
        pattern = jnp.where(sub == r, pick(weights, first + r), pattern)
    grad[width // LANES] = jnp.zeros((mix, LANES), F32)
    for low, high in tiles(width):
        n = high - low
        sq = blocks(s_ref[:, :n])
        own = blocks(own_ref[:, low:high].astype(F32))
        offset = own - blocks(truth[:, low:high])
        direct = lax.rsqrt(sums(offset * offset * sq, rows) + smoothing)
        g = offset * direct[None] - blocks(pair_ref[:, low:high]) * (1.0 / members)
        g = g * (sq * pattern[None, :, :n])
        grad[low // LANES, :, :n] = g.reshape(mix, n)
    last = width // LANES
    body, head = grad[last], grad[0]
    lane = lane_iota(body.shape)
    off = width - last * LANES
    wrapped = jnp.where(
        (lane >= off) & (lane < off + 2), pltpu.roll(head, off, 1), body
    )
    tail = pltpu.roll(body, LANES - off, 1)
    grad[last] = jnp.where(lane >= LANES - 2, tail, wrapped)
    for r in range(rows):
        for tile in range(lanes // LANES):
            g = grad[tile, pl.ds(r, channels, stride=rows), :]
            o_ref[r, :, tile * LANES : (tile + 1) * LANES] = g.astype(BF)


def over_lanes(h, shifted):
    rows, n, _ = shifted.shape
    s = shifted[...].reshape(rows * n, shifted.shape[2])[:, : h.shape[1]]
    return lax.dot_general(h, s, (((1,), (1,)), ((), ())), preferred_element_type=F32)


def kgrad_own_kernel(ksize, g_ref, own_ref, shift_ref, o_ref):
    rows, channels, lanes = g_ref.shape
    mid = ksize // 2
    for r in range(rows):
        g = g_ref[r].astype(F32)
        for b in range(ksize):
            moved = g if b == mid else pltpu.roll(g, (mid - b) % lanes, 1)
            shift_ref[r, b * channels : (b + 1) * channels] = moved.astype(BF)
        rest = shift_ref.shape[1] - ksize * channels
        shift_ref[r, ksize * channels :] = jnp.zeros((rest, lanes), BF)
    o_ref[...] = over_lanes(mixed(own_ref), shift_ref)


def kgrad_kernel(
    ksize, shift_ref, own_ref, near_ref, far_ref, keep_ref, give_ref, acc, total
):
    channels, rows = near_ref.shape[1:3]
    n = shift_ref.shape[1]
    odd = lax.axis_index("space") % 2
    mix = rows * channels
    both = over_lanes(
        jnp.concatenate([mixed(near_ref), mixed(far_ref)], axis=0), shift_ref
    )
    near, far = 2 * (1 - odd), 2 * odd
    core, half = lax.axis_index("core"), keep_ref.shape[0]
    for t in range(acc.shape[1]):
        lanes = slice(t * LANES, (t + 1) * LANES)
        acc[1, t] = own_ref[:, lanes]
        acc[near, t] = both[:mix, lanes]
        acc[far, t] = both[mix:, lanes]
    for i in range(ksize):
        for t in range(n // LANES):
            tap = None
            for r in range(rows):
                band, row = divmod(rows - ksize // 2 + r + i, rows)
                part = acc[
                    band, r * (n // LANES) + t, pl.ds(row, channels, stride=rows), :
                ]
                tap = part if tap is None else tap + part
            for h in range(2):
                low, high = max(i * channels, h * half), min((i + 1) * channels, (h + 1) * half)
                if low < high:
                    piece = tap[low - i * channels : high - i * channels]
                    total[
                        (h + core) % 2,
                        low - h * half : high - h * half,
                        t * LANES : (t + 1) * LANES,
                    ] = piece.astype(total.dtype)
    used = ksize * channels - half
    total[(1 + core) % 2, used:] = jnp.zeros((half - used, n), total.dtype)
    keep_ref[...] = total[0]
    give_ref[...] = total[1]


def gather_rows(own, near, far, scr):
    rows = scr.shape[0] // 3
    odd = lax.axis_index("space") % 2
    above, below = 2 * rows * (1 - odd), 2 * rows * odd
    for r in range(rows):
        scr[rows + r] = own(r)
        scr[above + r] = near(r)
        scr[below + r] = far(r)


def conv_kernel(ksize, w_ref, own_ref, near_ref, far_ref, o_ref, g_scr, tile_scr, mix_scr):
    rows, channels, lanes = own_ref.shape
    width = o_ref.shape[3]
    mid = ksize // 2
    gather_rows(
        lambda r: own_ref[r], lambda r: near_ref[r], lambda r: far_ref[r], g_scr
    )
    w = w_ref[...]
    for r in range(rows):
        g = g_scr[r : r + ksize].reshape(ksize * channels, lanes)
        y = jnp.dot(w, g, preferred_element_type=F32)
        out = None
        for b in range(ksize):
            part = y[b * channels : (b + 1) * channels]
            if b != mid:
                part = pltpu.roll(part, (mid - b) % lanes, 1)
            out = part if out is None else out + part
        for t in range(tile_scr.shape[0]):
            row = pl.ds(r, channels, stride=rows)
            tile_scr[t, row, :] = out[:, t * LANES : (t + 1) * LANES]
    for low, high in tiles(width):
        mix_scr[:, low:high] = tile_scr[low // LANES][:, : high - low].astype(BF)
    o_ref[0] = mix_scr[...].reshape(channels, rows, width)


def final_kernel(ksize, channels, norm, pieces, *refs):
    xs, (o_ref, scr, sem) = refs[: len(pieces)], refs[-3:]
    core = lax.axis_index("core")
    end = lax.axis_index("space") // 2
    n = xs[0].shape[0]
    for wait in (False, True):
        for k, (other, second) in enumerate(pieces):
            quarter = 2 * ((core + other) % 2) + (end + second) % 2
            for q in range(4):

                @pl.when(quarter == q)
                def _(k=k, q=q):
                    x_ref = xs[k]
                    slot = 0
                    for i in range(ksize):
                        low = max(i * channels, q * n)
                        high = min((i + 1) * channels, (q + 1) * n)
                        if low >= high:
                            continue
                        first = low - i * channels
                        at = (ksize - 1 - i, slice(None), pl.ds(first, high - low))
                        copy = pltpu.make_async_copy(
                            scr.at[at], o_ref.at[at], sem.at[k, slot]
                        )
                        slot += 1
                        if wait:
                            copy.wait()
                            continue
                        rows = slice(first, first + high - low)
                        for b in range(ksize):
                            x = x_ref[
                                low - q * n : high - q * n,
                                b * channels : (b + 1) * channels,
                            ]
                            scr[ksize - 1 - i, b, rows] = x.astype(F32) * norm
                        copy.start()


def flip(x, axis, bit):
    size = lax.axis_size(axis)
    return lax.ppermute(x, axis, [(i, i ^ bit) for i in range(size)])


def along(x):
    size = lax.axis_size("space")
    pairs = [(i, i + 2) for i in range(0, size - 2, 2)]
    pairs += [(i, i - 2) for i in range(3, size, 2)]
    return lax.ppermute(x, "space", pairs)


def across(x):
    size = lax.axis_size("space")
    pairs = [(i, i + 1) for i in range(1, size - 1, 2)]
    pairs += [(i, i - 1) for i in range(2, size, 2)]
    return lax.ppermute(x, "space", pairs)


def bits(axis):
    size, out = lax.axis_size(axis), []
    while (1 << len(out)) < size:
        out.append(1 << len(out))
    return out


def add(a, b):
    return (a.astype(F32) + b.astype(F32)).astype(BF)


def own_bit(axis, bit):
    return (lax.axis_index(axis) // bit) & 1


def halve(x, axis, bit):
    high = own_bit(axis, bit)
    n = x.shape[0] // 2
    keep = lax.dynamic_slice_in_dim(x, high * n, n, 0)
    give = lax.dynamic_slice_in_dim(x, (1 - high) * n, n, 0)
    return add(keep, flip(give, axis, bit))


def reduce_all(keep, give):
    core, first = ("core", 1), ("space", 2)
    x = add(keep, flip(give, *core))
    x = halve(x, *first)
    rest = [("space", b) for b in bits("space")[2:]]
    rest += [("chip", b) for b in bits("chip")] + [("space", 1)]
    for axis in rest:
        x = add(x, flip(x, *axis))
    y = flip(x, *first)
    x_other = flip(x, *core)
    y_other = flip(y, *core)
    return (x, y, x_other), (y_other,)


def body(prediction_maps, truth_analysis, reciprocal_spread, deconv_inputs, filter_tensor):
    channels, rows, width = prediction_maps.shape[1:]
    ksize = filter_tensor.shape[0]
    members = lax.axis_size("chip") * lax.axis_size("core")
    rows_total = rows * lax.axis_size("space")
    lanes = up(width + 4, LANES)
    span = truth_analysis.shape[1]
    sds = jax.ShapeDtypeStruct
    slab = sds((rows, channels, lanes), BF)

    def core(x):
        return flip(x, "core", 1)

    def spread(x):
        have = [x]
        for bit in bits("chip"):
            have += [flip(h, "chip", bit) for h in have]
        return have

    fields = spread(prediction_maps)
    near = flip(deconv_inputs, "space", 1)
    far = across(deconv_inputs)
    truth = truth_analysis.astype(BF)
    truths = spread(truth)
    mix = rows * channels
    scale, own = call(
        own_kernel,
        [sds((mix, LANES), F32), sds((mix, width), BF)],
        [reciprocal_spread[None], prediction_maps],
        [
            pltpu.VMEM((1, channels), F32),
            pltpu.VMEM((1, channels, rows, width), BF),
            pltpu.SemaphoreType.DMA((2,)),
        ],
        anywhere=[0, 1],
    )
    taps = jnp.transpose(filter_tensor, (1, 2, 0, 3)).reshape(ksize * channels, ksize * channels)
    arrived, seen = [], []
    for i, (x, t) in enumerate(zip(fields, truths)):
        arrived += [x, core(x)] if i else [core(x)]
        seen += [t, core(t)]

    table = [float(v) for v in area_weights(rows_total)]
    paired = call(
        functools.partial(pair_kernel, rows),
        [sds((mix, width), F32)],
        [scale, own, *arrived],
        [pltpu.VMEM((members - 1, mix, width), BF)],
        spare=max(3, members) << 20,
    )[0]
    grad = call(
        functools.partial(energy_kernel, span, members, table),
        [slab],
        [scale, own, paired, *seen],
        [
            pltpu.VMEM((members, channels, span), BF),
            pltpu.VMEM((mix, lanes), F32),
            pltpu.VMEM((lanes // LANES, mix, LANES), F32),
            pltpu.SemaphoreType.DMA((members,)),
        ],
        anywhere=range(3, 3 + members),
    )[0]

    grad_near = flip(grad, "space", 1)
    grad_far = along(grad_near)

    n = ksize * channels
    packed = up(n, LANES)
    flops = 2 * n * n * rows * lanes
    shifted, own_part = call(
        functools.partial(kgrad_own_kernel, ksize),
        [sds((rows, packed, lanes), BF), sds((mix, rows * packed), F32)],
        [grad, deconv_inputs],
        flops=flops // 3,
    )
    keep, give = call(
        functools.partial(kgrad_kernel, ksize),
        [sds((packed // 2, packed), BF)] * 2,
        [shifted, own_part, near, far],
        [
            pltpu.VMEM((3, rows * packed // LANES, mix, LANES), F32),
            pltpu.VMEM((2, packed // 2, packed), BF),
        ],
        flops * 2 // 3,
    )
    early, late = reduce_all(keep, give)

    grad_hidden = call(
        functools.partial(conv_kernel, ksize),
        [sds(prediction_maps.shape, BF)],
        [taps, grad, grad_near, grad_far],
        [
            pltpu.VMEM((3 * rows, channels, lanes), BF),
            pltpu.VMEM((lanes // LANES, mix, LANES), F32),
            pltpu.VMEM((mix, width), BF),
        ],
        2 * n * n * rows * lanes,
    )[0]

    norm = 1.0 / float(members * rows_total * width) ** 0.5
    shape = (ksize, ksize, channels, channels)

    def finish(pieces, *xs):
        count = len(pieces)
        return call(
            functools.partial(final_kernel, ksize, channels, norm, pieces),
            [sds(shape, F32)],
            xs,
            [pltpu.VMEM(shape, F32), pltpu.SemaphoreType.DMA((count, 3))],
            anywhere=range(count, len(xs)),
            outside=True,
            aliases={count: 0} if len(xs) > count else {},
        )[0]

    grad_kernel = finish([(0, 0), (0, 1), (1, 0)], *early)
    grad_kernel = finish([(1, 1)], *late, grad_kernel)
    return (grad_hidden, grad_kernel)


def solution(mesh):
    space, members = mesh.devices.shape
    fine = Mesh(
        mesh.devices.reshape(space, members // 2, 2), ("space", "chip", "core")
    )
    member = ("chip", "core")

    return jax.shard_map(
        body,
        mesh=fine,
        in_specs=(
            P(member, None, "space", None),
            P(None, ("space", *member)),
            P(),
            P(member, None, "space", None),
            P(),
        ),
        out_specs=(P(member, None, "space", None), P()),
        check_vma=False,
    )
```

```python
import functools
import math

import jax
import jax.numpy as jnp
import numpy as np
from jax import lax
from jax.experimental import pallas as pl
from jax.experimental.pallas import tpu as pltpu
from jax.sharding import Mesh, PartitionSpec as P


smoothing = 1.0
LANES = 128
BF = jnp.bfloat16
F32 = jnp.float32
VM = pl.BlockSpec(memory_space=pltpu.VMEM)
ANY = pl.BlockSpec(memory_space=pltpu.HBM)


def up(n, k):
    return -(-n // k) * k


def area_weights(rows_total):
    index = np.arange(rows_total)
    latitude = (index + 0.5) * (np.pi / rows_total) - np.pi / 2
    cosine = np.cos(latitude)
    return cosine / np.mean(cosine)


def call(kernel, outs, ins, scratch=(), flops=0, anywhere=(), outside=False, aliases={}, spare=3 << 20):
    nbytes = sum(x.size * x.dtype.itemsize for x in (*ins, *outs))
    held = sum(
        up(s.shape[-1], LANES) * math.prod(s.shape[:-1]) * s.dtype.itemsize
        for s in scratch
        if s.memory_space == pltpu.VMEM
    )
    return pl.pallas_call(
        kernel,
        out_shape=list(outs),
        in_specs=[ANY if i in anywhere else VM for i in range(len(ins))],
        out_specs=[ANY if outside else VM for _ in outs],
        scratch_shapes=list(scratch),
        input_output_aliases=aliases,
        cost_estimate=pl.CostEstimate(
            flops=flops, bytes_accessed=nbytes, transcendentals=0
        ),
        compiler_params=pltpu.CompilerParams(vmem_limit_bytes=held + spare),
    )(*ins)


def lane_iota(shape):
    return lax.broadcasted_iota(jnp.int32, shape, len(shape) - 1)


def mixed(ref):
    x = ref[0]
    return x.reshape(x.shape[0] * x.shape[1], x.shape[2])


def own_kernel(s_ref, x_ref, scale_ref, own_ref, s_scr, x_scr, sem):
    copies = [
        pltpu.make_async_copy(s_ref, s_scr, sem.at[0]),
        pltpu.make_async_copy(x_ref, x_scr, sem.at[1]),
    ]
    for copy in copies:
        copy.start()
    copies[0].wait()
    n, c = scale_ref.shape[0], s_ref.shape[1]
    i = lax.broadcasted_iota(jnp.int32, (n, c), 0)
    j = lax.broadcasted_iota(jnp.int32, (n, c), 1)
    s = jnp.broadcast_to(s_scr[...], (n, c))
    s = jnp.sum(jnp.where(i // (n // c) == j, s, 0.0), axis=1, keepdims=True)
    scale_ref[...] = jnp.broadcast_to(s * s, scale_ref.shape)
    copies[1].wait()
    own_ref[...] = mixed(x_scr)


def pick(table, index):
    out = jnp.float32(table[0])
    for i, v in enumerate(table[1:], 1):
        out = jnp.where(index == i, jnp.float32(v), out)
    return out


def sums(x, rows):
    x = jnp.sum(x, axis=0)
    step = rows
    while step < 8:
        x = x + pltpu.roll(x, step, 0)
        step *= 2
    return x


def tiles(width):
    return [(low, min(low + LANES, width)) for low in range(0, width, LANES)]


def blocks(x):
    return x.reshape(x.shape[0] // 8, 8, x.shape[1])


def pair_kernel(rows, s_ref, own_ref, *refs):
    *others, o_ref, mix_scr = refs
    for d, other in enumerate(others):
        mix_scr[d] = mixed(other)
    for low, high in tiles(mix_scr.shape[2]):
        sq = blocks(s_ref[:, : high - low])
        own = blocks(own_ref[:, low:high].astype(F32))
        self_inverse = 1.0 / jnp.sqrt(smoothing)
        total = jnp.full(own.shape[1:], self_inverse, F32)
        mixture = own * self_inverse
        for d in range(len(others)):
            other = blocks(mix_scr[d, :, low:high].astype(F32))
            diff = own - other
            inverse = lax.rsqrt(sums(diff * diff * sq, rows) + smoothing)
            total = total + inverse
            mixture = mixture + other * inverse[None]
        o_ref[:, low:high] = (own * total[None] - mixture).reshape(-1, high - low)


def energy_kernel(span, members, weights, s_ref, own_ref, pair_ref, *refs):
    truths = refs[:members]
    o_ref, part_scr, truth, grad, sem = refs[members:]
    rows, channels, lanes = o_ref.shape
    width = own_ref.shape[1]
    mix = channels * rows
    parts = members // rows
    me = lax.axis_index("chip") * 2 + lax.axis_index("core")
    first = lax.axis_index("space") * rows
    copies = [
        pltpu.make_async_copy(truths[d], part_scr.at[me ^ d], sem.at[d])
        for d in range(members)
    ]
    for copy in copies:
        copy.start()
    i = lax.broadcasted_iota(jnp.int32, (mix, channels), 0)
    j = lax.broadcasted_iota(jnp.int32, (mix, channels), 1)
    place = [(i == j * rows + r).astype(BF) for r in range(rows)]
    for copy in copies:
        copy.wait()
    for k in range(parts):
        truth[:, k * span : (k + 1) * span] = sum(
            jnp.dot(place[r], part_scr[r * parts + k], preferred_element_type=F32)
            for r in range(rows)
        )
    sub = lax.broadcasted_iota(jnp.int32, (8, LANES), 0) % rows
    pattern = jnp.full((8, LANES), pick(weights, first), F32)
    for r in range(1, rows):
        pattern = jnp.where(sub == r, pick(weights, first + r), pattern)
    grad[width // LANES] = jnp.zeros((mix, LANES), F32)
    for low, high in tiles(width):
        n = high - low
        sq = blocks(s_ref[:, :n])
        own = blocks(own_ref[:, low:high].astype(F32))
        offset = own - blocks(truth[:, low:high])
        direct = lax.rsqrt(sums(offset * offset * sq, rows) + smoothing)
        g = offset * direct[None] - blocks(pair_ref[:, low:high]) * (1.0 / members)
        g = g * (sq * pattern[None, :, :n])
        grad[low // LANES, :, :n] = g.reshape(mix, n)
    last = width // LANES
    body, head = grad[last], grad[0]
    lane = lane_iota(body.shape)
    off = width - last * LANES
    wrapped = jnp.where(
        (lane >= off) & (lane < off + 2), pltpu.roll(head, off, 1), body
    )
    tail = pltpu.roll(body, LANES - off, 1)
    grad[last] = jnp.where(lane >= LANES - 2, tail, wrapped)
    for r in range(rows):
        for tile in range(lanes // LANES):
            g = grad[tile, pl.ds(r, channels, stride=rows), :]
            o_ref[r, :, tile * LANES : (tile + 1) * LANES] = g.astype(BF)


def over_lanes(h, shifted):
    rows, n, _ = shifted.shape
    s = shifted[...].reshape(rows * n, shifted.shape[2])[:, : h.shape[1]]
    return lax.dot_general(h, s, (((1,), (1,)), ((), ())), preferred_element_type=F32)


def kgrad_own_kernel(ksize, g_ref, own_ref, shift_ref, o_ref):
    rows, channels, lanes = g_ref.shape
    mid = ksize // 2
    for r in range(rows):
        g = g_ref[r].astype(F32)
        for b in range(ksize):
            moved = g if b == mid else pltpu.roll(g, (mid - b) % lanes, 1)
            shift_ref[r, b * channels : (b + 1) * channels] = moved.astype(BF)
        rest = shift_ref.shape[1] - ksize * channels
        shift_ref[r, ksize * channels :] = jnp.zeros((rest, lanes), BF)
    o_ref[...] = over_lanes(mixed(own_ref), shift_ref)


def kgrad_kernel(ksize, shift_ref, own_ref, near_ref, far_ref, o_ref, acc):
    channels, rows = near_ref.shape[1:3]
    n = shift_ref.shape[1]
    odd = lax.axis_index("space") % 2
    mix = rows * channels
    both = over_lanes(
        jnp.concatenate([mixed(near_ref), mixed(far_ref)], axis=0), shift_ref
    )
    near, far = 2 * (1 - odd), 2 * odd
    for t in range(acc.shape[1]):
        lanes = slice(t * LANES, (t + 1) * LANES)
        acc[1, t] = own_ref[:, lanes]
        acc[near, t] = both[:mix, lanes]
        acc[far, t] = both[mix:, lanes]
    for i in range(ksize):
        for t in range(n // LANES):
            tap = None
            for r in range(rows):
                band, row = divmod(rows - ksize // 2 + r + i, rows)
                part = acc[
                    band, r * (n // LANES) + t, pl.ds(row, channels, stride=rows), :
                ]
                tap = part if tap is None else tap + part
            o_ref[
                i * channels : (i + 1) * channels, t * LANES : (t + 1) * LANES
            ] = tap.astype(o_ref.dtype)
    used = ksize * channels
    o_ref[used:] = jnp.zeros((o_ref.shape[0] - used, n), o_ref.dtype)


def gather_rows(own, near, far, scr):
    rows = scr.shape[0] // 3
    odd = lax.axis_index("space") % 2
    above, below = 2 * rows * (1 - odd), 2 * rows * odd
    for r in range(rows):
        scr[rows + r] = own(r)
        scr[above + r] = near(r)
        scr[below + r] = far(r)


def conv_kernel(ksize, w_ref, own_ref, near_ref, far_ref, o_ref, g_scr, tile_scr, mix_scr):
    rows, channels, lanes = own_ref.shape
    width = o_ref.shape[3]
    mid = ksize // 2
    gather_rows(
        lambda r: own_ref[r], lambda r: near_ref[r], lambda r: far_ref[r], g_scr
    )
    w = w_ref[...]
    for r in range(rows):
        g = g_scr[r : r + ksize].reshape(ksize * channels, lanes)
        y = jnp.dot(w, g, preferred_element_type=F32)
        out = None
        for b in range(ksize):
            part = y[b * channels : (b + 1) * channels]
            if b != mid:
                part = pltpu.roll(part, (mid - b) % lanes, 1)
            out = part if out is None else out + part
        for t in range(tile_scr.shape[0]):
            row = pl.ds(r, channels, stride=rows)
            tile_scr[t, row, :] = out[:, t * LANES : (t + 1) * LANES]
    for low, high in tiles(width):
        mix_scr[:, low:high] = tile_scr[low // LANES][:, : high - low].astype(BF)
    o_ref[0] = mix_scr[...].reshape(channels, rows, width)


def final_kernel(ksize, channels, norm, pieces, *refs):
    xs, (o_ref, scr, sem) = refs[: len(pieces)], refs[-3:]
    core = lax.axis_index("core")
    end = lax.axis_index("space") // 2
    n = xs[0].shape[0]
    for wait in (False, True):
        for k, (other, second) in enumerate(pieces):
            quarter = 2 * ((core + other) % 2) + (end + second) % 2
            for q in range(4):

                @pl.when(quarter == q)
                def _(k=k, q=q):
                    x_ref = xs[k]
                    slot = 0
                    for i in range(ksize):
                        low = max(i * channels, q * n)
                        high = min((i + 1) * channels, (q + 1) * n)
                        if low >= high:
                            continue
                        first = low - i * channels
                        at = (ksize - 1 - i, slice(None), pl.ds(first, high - low))
                        copy = pltpu.make_async_copy(
                            scr.at[at], o_ref.at[at], sem.at[k, slot]
                        )
                        slot += 1
                        if wait:
                            copy.wait()
                            continue
                        rows = slice(first, first + high - low)
                        for b in range(ksize):
                            x = x_ref[
                                low - q * n : high - q * n,
                                b * channels : (b + 1) * channels,
                            ]
                            scr[ksize - 1 - i, b, rows] = x.astype(F32) * norm
                        copy.start()


def flip(x, axis, bit):
    size = lax.axis_size(axis)
    return lax.ppermute(x, axis, [(i, i ^ bit) for i in range(size)])


def along(x):
    size = lax.axis_size("space")
    pairs = [(i, i + 2) for i in range(0, size - 2, 2)]
    pairs += [(i, i - 2) for i in range(3, size, 2)]
    return lax.ppermute(x, "space", pairs)


def across(x):
    size = lax.axis_size("space")
    pairs = [(i, i + 1) for i in range(1, size - 1, 2)]
    pairs += [(i, i - 1) for i in range(2, size, 2)]
    return lax.ppermute(x, "space", pairs)


def bits(axis):
    size, out = lax.axis_size(axis), []
    while (1 << len(out)) < size:
        out.append(1 << len(out))
    return out


def add(a, b):
    return (a.astype(F32) + b.astype(F32)).astype(BF)


def own_bit(axis, bit):
    return (lax.axis_index(axis) // bit) & 1


def halve(x, axis, bit):
    high = own_bit(axis, bit)
    n = x.shape[0] // 2
    keep = lax.dynamic_slice_in_dim(x, high * n, n, 0)
    give = lax.dynamic_slice_in_dim(x, (1 - high) * n, n, 0)
    return add(keep, flip(give, axis, bit))


def reduce_all(x):
    core, first = ("core", 1), ("space", 2)
    x = halve(x, *core)
    x = halve(x, *first)
    rest = [("space", b) for b in bits("space")[2:]]
    rest += [("space", 1)] + [("chip", b) for b in bits("chip")]
    for axis in rest:
        x = add(x, flip(x, *axis))
    y = flip(x, *first)
    x_other = flip(x, *core)
    y_other = flip(y, *core)
    return (x, y, x_other), (y_other,)


def body(prediction_maps, truth_analysis, reciprocal_spread, deconv_inputs, filter_tensor):
    channels, rows, width = prediction_maps.shape[1:]
    ksize = filter_tensor.shape[0]
    members = lax.axis_size("chip") * lax.axis_size("core")
    rows_total = rows * lax.axis_size("space")
    lanes = up(width + 4, LANES)
    span = truth_analysis.shape[1]
    sds = jax.ShapeDtypeStruct
    slab = sds((rows, channels, lanes), BF)

    def core(x):
        return flip(x, "core", 1)

    def spread(x):
        have = [x]
        for bit in bits("chip"):
            have += [flip(h, "chip", bit) for h in have]
        return have

    fields = spread(prediction_maps)
    near = flip(deconv_inputs, "space", 1)
    far = across(deconv_inputs)
    truth = truth_analysis.astype(BF)
    truths = spread(truth)
    mix = rows * channels
    scale, own = call(
        own_kernel,
        [sds((mix, LANES), F32), sds((mix, width), BF)],
        [reciprocal_spread[None], prediction_maps],
        [
            pltpu.VMEM((1, channels), F32),
            pltpu.VMEM((1, channels, rows, width), BF),
            pltpu.SemaphoreType.DMA((2,)),
        ],
        anywhere=[0, 1],
    )
    taps = jnp.transpose(filter_tensor, (1, 2, 0, 3)).reshape(ksize * channels, ksize * channels)
    arrived, seen = [], []
    for i, (x, t) in enumerate(zip(fields, truths)):
        arrived += [x, core(x)] if i else [core(x)]
        seen += [t, core(t)]

    table = [float(v) for v in area_weights(rows_total)]
    paired = call(
        functools.partial(pair_kernel, rows),
        [sds((mix, width), F32)],
        [scale, own, *arrived],
        [pltpu.VMEM((members - 1, mix, width), BF)],
        spare=max(3, members) << 20,
    )[0]
    grad = call(
        functools.partial(energy_kernel, span, members, table),
        [slab],
        [scale, own, paired, *seen],
        [
            pltpu.VMEM((members, channels, span), BF),
            pltpu.VMEM((mix, lanes), F32),
            pltpu.VMEM((lanes // LANES, mix, LANES), F32),
            pltpu.SemaphoreType.DMA((members,)),
        ],
        anywhere=range(3, 3 + members),
    )[0]

    grad_near = flip(grad, "space", 1)
    grad_far = along(grad_near)

    n = ksize * channels
    packed = up(n, LANES)
    flops = 2 * n * n * rows * lanes
    shifted, own_part = call(
        functools.partial(kgrad_own_kernel, ksize),
        [sds((rows, packed, lanes), BF), sds((mix, rows * packed), F32)],
        [grad, deconv_inputs],
        flops=flops // 3,
    )
    partial = call(
        functools.partial(kgrad_kernel, ksize),
        [sds((packed, packed), BF)],
        [shifted, own_part, near, far],
        [pltpu.VMEM((3, rows * packed // LANES, mix, LANES), F32)],
        flops * 2 // 3,
    )[0]
    early, late = reduce_all(partial)

    grad_hidden = call(
        functools.partial(conv_kernel, ksize),
        [sds(prediction_maps.shape, BF)],
        [taps, grad, grad_near, grad_far],
        [
            pltpu.VMEM((3 * rows, channels, lanes), BF),
            pltpu.VMEM((lanes // LANES, mix, LANES), F32),
            pltpu.VMEM((mix, width), BF),
        ],
        2 * n * n * rows * lanes,
    )[0]

    norm = 1.0 / float(members * rows_total * width) ** 0.5
    shape = (ksize, ksize, channels, channels)

    def finish(pieces, *xs):
        count = len(pieces)
        return call(
            functools.partial(final_kernel, ksize, channels, norm, pieces),
            [sds(shape, F32)],
            xs,
            [pltpu.VMEM(shape, F32), pltpu.SemaphoreType.DMA((count, 3))],
            anywhere=range(count, len(xs)),
            outside=True,
            aliases={count: 0} if len(xs) > count else {},
        )[0]

    grad_kernel = finish([(0, 0), (0, 1), (1, 0)], *early)
    grad_kernel = finish([(1, 1)], *late, grad_kernel)
    return (grad_hidden, grad_kernel)


def solution(mesh):
    space, members = mesh.devices.shape
    fine = Mesh(
        mesh.devices.reshape(space, members // 2, 2), ("space", "chip", "core")
    )
    member = ("chip", "core")

    return jax.shard_map(
        body,
        mesh=fine,
        in_specs=(
            P(member, None, "space", None),
            P(None, ("space", *member)),
            P(),
            P(member, None, "space", None),
            P(),
        ),
        out_specs=(P(member, None, "space", None), P()),
        check_vma=False,
    )
```
